128 devices in a mesh: leaf: 4 (over y), row: 4 (over z), col: 8 (over x, core).
Axes of the slice: x: 4, y: 4, z: 4, core: 2. Of those that a mesh axis runs over, the one named last changes fastest.
Arguments:
- rhs_leaf: bfloat16 [4, 12288, 256], P('leaf', 'col'), may hold values from -6 to 6
- rhs_parent: bfloat16 [16384, 256], P(('leaf', 'row', 'col')), may hold values from -6 to 6
- inv_leaf: bfloat16 [4, 12288, 12288], P('leaf', 'row', 'col'), as said below
- panel: bfloat16 [4, 6144, 12288], P('leaf', 'col', 'row'), may hold values from -0.0546875 to 0.0546875
- row_map: int32 [4, 6144], P('leaf', 'col'), may hold values from 0 to 16383, as said below
- inv_parent: bfloat16 [16384, 16384], P(('row', 'col'), 'leaf'), as said below
Outputs:
- sol_leaf: bfloat16 [4, 12288, 256], P('leaf', 'col')
- sol_parent: bfloat16 [16384, 256], P(('leaf', 'row', 'col'))
The draws below stay inside these ranges and needn't reach their ends.
Inputs may be any that keep to these rules, and one draw needn't show every extreme that they name: Within one leaf the 6144 entries of row_map are distinct parent rows. Split the parent rows into 128 owner blocks of 16384 // 128 consecutive rows: in each aligned block of 192 consecutive entries of a leaf, at most 2 entries fall in one owner block, and exactly 2 in some. `inv_leaf`: lower triangular: zeros above the diagonal, diagonal entries between 0.5 and 2. `inv_parent`: lower triangular: zeros above the diagonal, diagonal entries between 0.5 and 2.
All inputs are finite; a program needn't handle non-finite values.
Results may differ from the reference program's by a relative error of at most 0.01.
Values may be sent and summed in bfloat16 or wider, within the bound.
A program may use at most 128 MiB of HBM per device.

```python
import jax
import jax.numpy as jnp

NL = 12288
NA = 6144
NP = 16384
R = 256
LEAVES = 4
DEVICES = 128


def triangle(key, order):
    lower_key, diag_key = jax.random.split(key)
    rows = jnp.arange(order)[:, None]
    cols = jnp.arange(order)[None, :]
    entries = jax.random.normal(lower_key, (order, order), jnp.float32)
    entries = entries * order ** (-0.5)
    diagonal = jax.random.uniform(diag_key, (order,), jnp.float32, 0.5, 2.0)
    lower = jnp.where(cols < rows, entries, 0.0)
    return lower + jnp.where(cols == rows, diagonal[:, None], 0.0)


def draw_inv_leaf(key, part):
    blocks = [triangle(jax.random.fold_in(key, member), NL) for member in range(LEAVES)]
    return jnp.stack(blocks).astype(jnp.bfloat16)


def draw_inv_parent(key, part):
    return triangle(jax.random.fold_in(key, 77), NP).astype(jnp.bfloat16)


def leaf_map(key, member):
    owned = NP // DEVICES
    owners = jax.random.permutation(jax.random.fold_in(key, member), DEVICES)
    offsets = jax.random.randint(jax.random.fold_in(key, 1000 + member), (DEVICES,), 0, owned)
    position = jnp.arange(NA)
    owner_index = owners[position % DEVICES]
    local_row = (position // DEVICES + offsets[owner_index]) % owned
    return owner_index * owned + local_row


def draw_row_map(key, part):
    maps = [leaf_map(key, member) for member in range(LEAVES)]
    return jnp.stack(maps).astype(jnp.int32)


def block_levels(key, shape, shards, low, largest):
    gain, own = 1.0, jax.random.fold_in(key, 6)
    for axis_at, blocks in shards:
        draws = jnp.exp(jax.random.uniform(jax.random.fold_in(own, axis_at), (blocks,), jnp.float32, low / len(shards), largest / len(shards)))
        gain = gain * jnp.repeat(draws, shape[axis_at] // blocks).reshape([-1 if axis == axis_at else 1 for axis in range(len(shape))])
    return gain


def gaussian(own_key, dims, deviation, limit, shards=(), held_as=jnp.bfloat16):
    values = jax.random.normal(own_key, dims, jnp.float32) * deviation
    if len(shards) > 0:
        values = block_levels(own_key, dims, shards, -0.22, 0.18) * values
    return jnp.clip(values, min=-limit, max=limit).astype(held_as)


def setup_inputs(seed: int = 0) -> dict:
    keys = jax.random.split(jax.random.key(seed), 7)
    return {
        "rhs_leaf": gaussian(keys[0], (LEAVES, NL, R), 1.0, 6.0, ((0, 4), (1, 8))),
        "rhs_parent": gaussian(keys[1], (NP, R), 1.0, 6.0, ((0, 128),)),
        "inv_leaf": draw_inv_leaf(jax.random.fold_in(keys[6], 71), 0),
        "panel": gaussian(keys[3], (LEAVES, NA, NL), NL ** -0.5, 0.0546875, ((0, 4), (1, 8), (2, 4))),
        "row_map": draw_row_map(jax.random.fold_in(keys[6], 71), 0),
        "inv_parent": draw_inv_parent(jax.random.fold_in(keys[6], 71), 0),
    }


def reference(rhs_leaf, rhs_parent, inv_leaf, panel, row_map, inv_parent):
    forward = []
    acc = rhs_parent.astype(jnp.float32)
    for member in range(LEAVES):
        solved = jnp.dot(inv_leaf[member], rhs_leaf[member], preferred_element_type=jnp.float32).astype(jnp.bfloat16)
        forward.append(solved)
        update = jnp.dot(panel[member], solved, preferred_element_type=jnp.float32)
        acc = acc.at[row_map[member]].add(-update)
    reduced = acc.astype(jnp.bfloat16)
    fwd_parent = jnp.dot(inv_parent, reduced, preferred_element_type=jnp.float32).astype(jnp.bfloat16)
    sol_parent = jnp.dot(inv_parent.T, fwd_parent, preferred_element_type=jnp.float32).astype(jnp.bfloat16)
    results = []
    for member in range(LEAVES):
        picked = sol_parent[row_map[member]]
        coupling = jnp.dot(panel[member].T, picked, preferred_element_type=jnp.float32)
        corrected = (forward[member].astype(jnp.float32) - coupling).astype(jnp.bfloat16)
        results.append(jnp.dot(inv_leaf[member].T, corrected, preferred_element_type=jnp.float32).astype(jnp.bfloat16))
    return jnp.stack(results), sol_parent
```

```python
import jax
import jax.numpy as jnp
from jax import lax
from jax.experimental import pallas as pl
from jax.experimental.pallas import tpu as pltpu
from jax.sharding import PartitionSpec as P

MESH = pl.DeviceIdType.MESH
BF = jnp.bfloat16
F32 = jnp.float32


def dot(a, b):
    return jnp.dot(a, b, preferred_element_type=F32)


class Comm:
    def __init__(self, ssem, rsem):
        self.ssem, self.rsem, self.n, self.sent = ssem, rsem, 0, []
        self.l, self.r, self.c = (lax.axis_index(a) for a in ("leaf", "row", "col"))
        self.x, self.k = self.c // 2, self.c % 2

    def at(self, axis, delta):
        if axis == "x":
            return (self.l, self.r, ((self.x + delta + 4) % 4) * 2 + self.k)
        if axis == "z":
            return (self.l, (self.r + delta + 4) % 4, self.c)
        if axis == "y":
            return ((self.l + delta + 4) % 4, self.r, self.c)
        return (self.l, self.r, self.x * 2 + 1 - self.k)

    def make(self, src, dst, device):
        at = self.n
        self.n += 1
        return pltpu.make_async_remote_copy(
            src_ref=src,
            dst_ref=dst,
            send_sem=self.ssem.at[at],
            recv_sem=self.rsem.at[at],
            device_id=device,
            device_id_type=MESH,
        )

    def send(self, src, dst, axis, delta=0):
        copy = self.make(src, dst, self.at(axis, delta))
        copy.start()
        self.sent.append(copy)
        return copy

    def drain(self):
        for copy in self.sent:
            copy.wait_send()
        self.sent = []


class RingSum:
    def __init__(self, comm, axis, q, slot):
        self.comm, self.axis, self.q, self.slot = comm, axis, q, slot

    def far(self):
        send, q, slot, axis = self.comm.send, self.q, self.slot, self.axis
        self.c0 = send(q(2, 0), slot(0), axis, 1)
        self.c1 = send(q(2, 1), slot(1), axis, -1)

    def near(self):
        send, q, slot, axis = self.comm.send, self.q, self.slot, self.axis
        self.c5 = send(q(1, 1), slot(5), axis, 1)
        self.c4 = send(q(3, 0), slot(4), axis, -1)

    def relay(self):
        send, q, slot, axis = self.comm.send, self.q, self.slot, self.axis
        self.c0.wait_recv()
        q(1, 0)[...] = (q(1, 0)[...].astype(F32) + slot(0)[...].astype(F32)).astype(BF)
        self.c2 = send(q(1, 0), slot(2), axis, 1)
        self.c1.wait_recv()
        q(3, 1)[...] = (q(3, 1)[...].astype(F32) + slot(1)[...].astype(F32)).astype(BF)
        self.c3 = send(q(3, 1), slot(3), axis, -1)

    def total(self, own0, own1):
        slot = self.slot
        self.c4.wait_recv()
        self.c2.wait_recv()
        a = own0 + slot(4)[...].astype(F32) + slot(2)[...].astype(F32)
        self.c5.wait_recv()
        self.c3.wait_recv()
        b = own1 + slot(5)[...].astype(F32) + slot(3)[...].astype(F32)
        return a, b

    def run(self):
        self.far()
        self.near()
        self.relay()


class RingGather:
    def __init__(self, comm, axis, me, g):
        self.comm, self.axis, self.me, self.g = comm, axis, me, g
        send = comm.send
        self.a_up = send(g(me, 0), g(me, 0), axis, 1)
        self.b_dn = send(g(me, 1), g(me, 1), axis, -1)
        self.b_up = send(g(me, 1), g(me, 1), axis, 1)
        self.a_dn = send(g(me, 0), g(me, 0), axis, -1)
        self.prev, self.next, self.opp = (me + 3) % 4, (me + 1) % 4, (me + 2) % 4

    def relay(self):
        send, g = self.comm.send, self.g
        self.a_up.wait_recv()
        self.a_far = send(g(self.prev, 0), g(self.prev, 0), self.axis, 1)
        self.b_dn.wait_recv()
        self.b_far = send(g(self.next, 1), g(self.next, 1), self.axis, -1)

    def near(self):
        self.b_up.wait_recv()
        self.a_dn.wait_recv()

    def far(self):
        self.a_far.wait_recv()
        self.b_far.wait_recv()

    def run(self):
        self.relay()
        self.near()
        self.far()


def kernel(
    x_hbm, rp_hbm, a_hbm, b_hbm, p_hbm, rm_ref,
    out_ref, solp_ref,
    a_v, b_v, p_v, x_v, rp_v,
    sb1, rb1, q1, own1, rr1, y_v, yt,
    u_acc, q2, rr2,
    g_v, r1_v, r2_v, qs, qr, t1, t1t, s1, s1t,
    q3, rr3, gred, q4, rr4, ft,
    sb5, rb5, q5, own5, rz0, rx0, rx1, rz1,
    sp, pk, sb7, rb7, q7, own7, rr7, ct,
    acc8, q8, rr8,
    ssem, rsem, lsem, asem, bsem,
):
    cm = Comm(ssem, rsem)
    l, r, c, x, k = cm.l, cm.r, cm.c, cm.x, cm.k
    me = r * 8 + c
    n8 = y_v.shape[2]
    R = x_v.shape[1]
    H = R // 2
    own = rp_v.shape[0]
    blk = s1t.shape[0]

    loads = [pltpu.make_async_copy(x_hbm, x_v, lsem.at[0])]
    for i, d in enumerate((2, 3, 1, 0)):
        for j, core in enumerate((1 - k, k)):
            rows = pl.ds(pl.multiple_of((((x + d) % 4) * 2 + core) * n8, n8), n8)
            loads.append(pltpu.make_async_copy(a_hbm.at[rows], a_v.at[rows], lsem.at[1 + 2 * i + j]))
    loads.append(pltpu.make_async_copy(rp_hbm, rp_v, lsem.at[9]))
    loads.append(pltpu.make_async_copy(b_hbm, b_v, lsem.at[10]))
    loads.append(pltpu.make_async_copy(p_hbm, p_v, lsem.at[11]))
    for load in loads:
        load.start()

    barrier = pltpu.get_barrier_semaphore()

    def greet(n, _):
        to = (me + n) % 32
        pl.semaphore_signal(barrier, inc=1, device_id=(l, to // 8, to % 8), device_id_type=MESH)
        return 0

    lax.fori_loop(1, 32, greet, 0)
    for d in (1, 3):
        pl.semaphore_signal(barrier, inc=1, device_id=((l + d) % 4, r, c), device_id_type=MESH)

    shift = own.bit_length() - 1
    e = rm_ref[pl.ds(r, 1), :]
    owner = lax.shift_right_logical(e, shift)
    local = lax.bitwise_and(e, own - 1).astype(F32)
    across = jnp.broadcast_to(owner.astype(F32), (blk, blk))
    down = across.T
    before = lax.broadcasted_iota(jnp.int32, (blk, blk), 0) < lax.broadcasted_iota(jnp.int32, (blk, blk), 1)
    rank = jnp.sum(jnp.where((across == down) & before, 1.0, 0.0), axis=0, keepdims=True)
    place = lax.bitwise_and(owner, 31) * 8 + lax.shift_right_logical(owner, 5) * 2
    place = place.astype(F32) + rank
    pick = jnp.where(
        lax.broadcasted_iota(jnp.int32, (256, blk), 0).astype(F32) == jnp.broadcast_to(place, (256, blk)), 1.0, 0.0
    )
    s1[...] = pick.astype(BF)
    s1t[...] = pick.T.astype(BF)
    qv = jnp.sum(pick * jnp.broadcast_to(local + 1.0, (256, blk)), axis=1, keepdims=True)
    qs[...] = jnp.broadcast_to(qv, (256, own)).reshape(32, 8, own)
    qr[pl.ds(me, 1)] = qs[pl.ds(me, 1)]

    pl.semaphore_wait(barrier, 33)

    def plane_exchange(src, dst, which):
        def one(n, _):
            to = (me + n) % 32
            pltpu.make_async_remote_copy(
                src_ref=src.at[to], dst_ref=dst.at[me], send_sem=asem.at[which], recv_sem=bsem.at[which],
                device_id=(l, to // 8, to % 8), device_id_type=MESH,
            ).start()
            return 0

        lax.fori_loop(1, 32, one, 0)

    def plane_wait(src, dst, which):
        copy = pltpu.make_async_remote_copy(
            src_ref=src.at[pl.ds(0, 31)], dst_ref=dst.at[pl.ds(0, 31)], send_sem=asem.at[which],
            recv_sem=bsem.at[which], device_id=cm.at("c", 0), device_id_type=MESH,
        )
        copy.wait_send()
        copy.wait_recv()

    plane_exchange(qs, qr, 0)

    loads[0].wait()
    xv = x_v[...]
    half = n8 // 2
    sib = {}

    def a_rows(d, core):
        return pl.ds(pl.multiple_of((((x + d) % 4) * 2 + core) * n8, n8), n8)

    ring = RingSum(cm, "x", lambda d, h: q1.at[d, pl.ds(h * half, half)], lambda i: rr1.at[i])
    for i, d in enumerate((2, 3, 1, 0)):
        loads[1 + 2 * i].wait()
        sb1[d] = dot(a_v[a_rows(d, 1 - k), :], xv).astype(BF)
        sib[d] = cm.send(sb1.at[d], rb1.at[d], "c")
    for i, d in enumerate((2, 3, 1, 0)):
        loads[2 + 2 * i].wait()
        part = dot(a_v[a_rows(d, k), :], xv)
        sib[d].wait_recv()
        part = part + rb1[d].astype(F32)
        if d:
            q1[d] = part.astype(BF)
        else:
            own1[...] = part
        if d == 2:
            ring.far()
        if d == 1:
            ring.near()
    ring.relay()
    a, b = ring.total(own1[:half], own1[half:])
    y_v[x, k, :half] = a.astype(BF)
    y_v[x, k, half:] = b.astype(BF)

    gat = RingGather(cm, "x", x, lambda i, h: y_v.at[i, k, pl.ds(h * half, half)])
    fwd = [cm.send(y_v.at[x, k], y_v.at[x, k], "c")]
    yt[:, :half] = a.T.astype(BF)
    yt[:, half:] = b.T.astype(BF)
    loads[10].wait()

    def panel_cols(xx, core):
        return pl.ds(pl.multiple_of((xx * 2 + core) * n8, n8), n8)

    def push(xx, core, first=False):
        part = dot(b_v[:, panel_cols(xx, core)], y_v[xx, core])
        u_acc[...] = part if first else u_acc[...] + part

    push(x, k, True)
    gat.relay()
    gat.near()
    fwd.append(cm.send(y_v.at[gat.prev, k], y_v.at[gat.prev, k], "c"))
    fwd.append(cm.send(y_v.at[gat.next, k], y_v.at[gat.next, k], "c"))
    fwd[0].wait_recv()
    push(x, 1 - k)
    push(gat.prev, k)
    push(gat.next, k)
    gat.far()
    fwd.append(cm.send(y_v.at[gat.opp, k], y_v.at[gat.opp, k], "c"))
    fwd[1].wait_recv()
    push(gat.prev, 1 - k)
    fwd[2].wait_recv()
    push(gat.next, 1 - k)
    push(gat.opp, k)
    fwd[3].wait_recv()
    push(gat.opp, 1 - k)

    plane_wait(qs, qr, 0)
    seen = qr[...].reshape(256, own)
    lane = lax.broadcasted_iota(jnp.int32, (256, own), 1).astype(F32) + 1.0
    leaf_of = lax.bitwise_and(
        lax.shift_right_logical(lax.broadcasted_iota(jnp.int32, (256, own), 0), 1), 3
    )
    for i in range(4):
        table = jnp.where((seen == lane) & (leaf_of == i), 1.0, 0.0)
        t1t[:, i * own : (i + 1) * own] = table.astype(BF)
        t1[i * own : (i + 1) * own, :] = table.T.astype(BF)

    quarter = blk // 2

    def u_rows(d):
        return u_acc[pl.ds(pl.multiple_of(((r + d) % 4) * blk, blk), blk), :]

    for d in (2, 1, 3):
        q2[d] = u_rows(d).astype(BF)
    ring = RingSum(cm, "z", lambda d, h: q2.at[d, pl.ds(h * quarter, quarter)], lambda i: rr2.at[i])
    ring.run()
    mine = u_rows(0)
    a, b = ring.total(mine[:quarter], mine[quarter:])
    q2[0, :quarter] = a.astype(BF)
    q2[0, quarter:] = b.astype(BF)

    g_v[...] = dot(s1[...], q2[0]).reshape(32, 8, R)
    r1_v[pl.ds(me, 1)] = g_v[pl.ds(me, 1)]
    plane_exchange(g_v, r1_v, 1)
    plane_wait(g_v, r1_v, 1)
    got = r1_v[...].reshape(256, R).astype(BF)
    hown = own // 2

    def t_rows(d):
        return t1[pl.ds(pl.multiple_of(((l + d) % 4) * own, own), own), :]

    for d in (2, 1, 3):
        q3[d] = dot(t_rows(d), got).astype(BF)
    ring = RingSum(cm, "y", lambda d, h: q3.at[d, pl.ds(h * hown, hown)], lambda i: rr3.at[i])
    ring.far()
    ring.near()
    mine = dot(t_rows(0), got)
    ring.relay()
    a, b = ring.total(mine[:hown], mine[hown:])
    loads[9].wait()
    rp = rp_v[...].astype(F32)
    for h in range(2):
        cols = slice(h * H, (h + 1) * H)
        gred[h, r, x, k, :hown] = (rp[:hown, cols] - a[:, cols]).astype(BF)
        gred[h, r, x, k, hown:] = (rp[hown:, cols] - b[:, cols]).astype(BF)

    g0 = RingGather(cm, "x", x, lambda i, h: gred.at[0, r, i, k, pl.ds(h * hown, hown)])
    g1 = RingGather(cm, "z", r, lambda i, h: gred.at[1, i, x, k, pl.ds(h * hown, hown)])
    g0.relay()
    g1.relay()
    g0.near()
    g0.far()
    g1.near()
    g1.far()
    g2 = RingGather(cm, "z", r, lambda i, h: gred.at[0, i, pl.ds(2 * h, 2), k])
    g3 = RingGather(cm, "x", x, lambda i, h: gred.at[1, pl.ds(2 * h, 2), i, k])
    fwd = [cm.send(gred.at[0, r, :, k], gred.at[0, r, :, k], "c")]
    fwd.append(cm.send(gred.at[1, :, x, k], gred.at[1, :, x, k], "c"))
    g2.relay()
    g3.relay()
    g2.near()
    fwd += [cm.send(gred.at[0, i, :, k], gred.at[0, i, :, k], "c") for i in (g2.prev, g2.next)]
    g3.near()
    fwd += [cm.send(gred.at[1, :, i, k], gred.at[1, :, i, k], "c") for i in (g3.prev, g3.next)]
    g2.far()
    fwd.append(cm.send(gred.at[0, g2.opp, :, k], gred.at[0, g2.opp, :, k], "c"))
    g3.far()
    fwd.append(cm.send(gred.at[1, :, g3.opp, k], gred.at[1, :, g3.opp, k], "c"))
    for copy in fwd:
        copy.wait_recv()

    loads[11].wait()
    parent = None
    for i in range(4):
        rhs = jnp.concatenate([gred[h, i].reshape(8 * own, H) for h in range(2)], axis=1)
        part = dot(p_v[:, i * 8 * own : (i + 1) * 8 * own], rhs)
        parent = part if parent is None else parent + part
    u_acc[: 4 * own] = parent

    def f_rows(d):
        return u_acc[pl.ds(pl.multiple_of(((l + d) % 4) * own, own), own), :]

    for d in (2, 1, 3):
        q4[d] = f_rows(d).astype(BF)
    ring = RingSum(cm, "y", lambda d, h: q4.at[d, pl.ds(h * hown, hown)], lambda i: rr4.at[i])
    ring.run()
    mine = f_rows(0)
    a, b = ring.total(mine[:hown], mine[hown:])
    fp = jnp.concatenate([a, b], axis=0)
    ft[l] = fp.T.astype(BF)
    gat = RingGather(cm, "y", l, lambda i, h: ft.at[i, pl.ds(h * H, H)])
    gat.run()

    lhs = jnp.concatenate([ft[i] for i in range(4)], axis=1)
    sib = {}
    for dr in (2, 3, 1, 0):
        for dx in range(4):
            at = ((r + dr) % 4) * 4 + (x + dx) % 4
            part = dot(lhs, p_v[:, pl.ds(pl.multiple_of(at * 2 * own, 2 * own), 2 * own)])
            lo, hi = part[:, :own], part[:, own:]
            mine = jnp.where(k == 0, lo, hi)
            sib_part = jnp.where(k == 0, hi, lo).astype(BF)
            for h in range(2):
                own5[h, dr, dx] = mine[h * H : (h + 1) * H]
                sb5[h, dr, dx] = sib_part[h * H : (h + 1) * H]
        sib[dr] = cm.send(sb5.at[:, dr], rb5.at[:, dr], "c")
    for dr in (2, 3, 1, 0):
        sib[dr].wait_recv()
        own5[:, dr] = own5[:, dr] + rb5[:, dr].astype(F32)
        q5[:, dr] = own5[:, dr].astype(BF)
    s0 = RingSum(cm, "z", lambda d, h: q5.at[0, d, pl.ds(2 * h, 2)], lambda i: rz0.at[i])
    s1x = RingSum(cm, "x", lambda d, h: q5.at[1, pl.ds(2 * h, 2), d], lambda i: rx1.at[i])
    s0.far()
    s1x.far()
    s0.near()
    s1x.near()
    s0.relay()
    s1x.relay()
    a0, b0 = s0.total(own5[0, 0, :2], own5[0, 0, 2:])
    a1, b1 = s1x.total(own5[1, :2, 0], own5[1, 2:, 0])
    q5[0, 0, :2] = a0.astype(BF)
    q5[0, 0, 2:] = b0.astype(BF)
    q5[1, :2, 0] = a1.astype(BF)
    q5[1, 2:, 0] = b1.astype(BF)
    hh = H // 2
    s2 = RingSum(cm, "x", lambda d, h: q5.at[0, 0, d, pl.ds(h * hh, hh)], lambda i: rx0.at[i])
    s3 = RingSum(cm, "z", lambda d, h: q5.at[1, d, 0, pl.ds(h * hh, hh)], lambda i: rz1.at[i])
    s2.far()
    s3.far()
    s2.near()
    s3.near()
    s2.relay()
    s3.relay()
    p0, p1 = s2.total(a0[0, :hh], a0[0, hh:])
    p2, p3 = s3.total(a1[0, :hh], a1[0, hh:])
    solved = jnp.concatenate([p0, p1, p2, p3], axis=0).T.astype(BF)
    solp_ref[...] = solved
    sp[l] = solved

    gat = RingGather(cm, "y", l, lambda i, h: sp.at[i, pl.ds(h * hown, hown)])
    gat.run()
    g2_v = g_v
    g2_v[...] = dot(t1t[...], sp[...].reshape(4 * own, R)).reshape(32, 8, R)
    r2_v[pl.ds(me, 1)] = g2_v[pl.ds(me, 1)]
    plane_exchange(g2_v, r2_v, 2)
    plane_wait(g2_v, r2_v, 2)
    pk[r] = dot(s1t[...], r2_v[...].reshape(256, R).astype(BF)).astype(BF)
    gat = RingGather(cm, "z", r, lambda i, h: pk.at[i, pl.ds(h * quarter, quarter)])
    gat.run()
    picked = pk[...].reshape(4 * blk, R).astype(F32).T.astype(BF)

    sib = {}
    ring = RingSum(cm, "x", lambda d, h: q7.at[d, pl.ds(h * H, H)], lambda i: rr7.at[i])
    for d in (2, 3, 1, 0):
        sb7[d] = dot(picked, b_v[:, panel_cols((x + d) % 4, 1 - k)]).astype(BF)
        sib[d] = cm.send(sb7.at[d], rb7.at[d], "c")
    for d in (2, 3, 1, 0):
        part = dot(picked, b_v[:, panel_cols((x + d) % 4, k)])
        sib[d].wait_recv()
        part = part + rb7[d].astype(F32)
        if d:
            q7[d] = part.astype(BF)
        else:
            own7[...] = part
        if d == 2:
            ring.far()
        if d == 1:
            ring.near()
    ring.relay()
    a, b = ring.total(own7[:H], own7[H:])
    ct[x, k, :H] = (yt[:H].astype(F32) - a).astype(BF)
    ct[x, k, H:] = (yt[H:].astype(F32) - b).astype(BF)

    gat = RingGather(cm, "x", x, lambda i, h: ct.at[i, k, pl.ds(h * H, H)])
    fwd = [cm.send(ct.at[x, k], ct.at[x, k], "c")]

    def pull(xx, core, first=False):
        lhs = ct[xx, core]
        rows = pl.ds(pl.multiple_of((xx * 2 + core) * n8, n8), n8)
        for d in (2, 1, 3, 0):
            cols = pl.ds(pl.multiple_of(((r + d) % 4) * n8, n8), n8)
            part = dot(lhs, a_v[rows, cols])
            acc8[d] = part if first else acc8[d] + part

    pull(x, k, True)
    gat.relay()
    gat.near()
    fwd.append(cm.send(ct.at[gat.prev, k], ct.at[gat.prev, k], "c"))
    fwd.append(cm.send(ct.at[gat.next, k], ct.at[gat.next, k], "c"))
    fwd[0].wait_recv()
    pull(x, 1 - k)
    pull(gat.prev, k)
    pull(gat.next, k)
    gat.far()
    fwd.append(cm.send(ct.at[gat.opp, k], ct.at[gat.opp, k], "c"))
    fwd[1].wait_recv()
    pull(gat.prev, 1 - k)
    fwd[2].wait_recv()
    pull(gat.next, 1 - k)
    pull(gat.opp, k)
    fwd[3].wait_recv()
    pull(gat.opp, 1 - k)
    for d in (2, 1, 3):
        q8[d] = acc8[d].astype(BF)
    ring = RingSum(cm, "z", lambda d, h: q8.at[d, pl.ds(h * H, H)], lambda i: rr8.at[i])
    ring.run()
    a, b = ring.total(acc8[0, :H], acc8[0, H:])
    out_ref[r] = jnp.concatenate([a, b], axis=0).T.astype(BF)
    gat = RingGather(cm, "z", r, lambda i, h: out_ref.at[i, pl.ds(h * half, half)])
    gat.run()
    cm.drain()


def per_device(rhs_leaf, rhs_parent, inv_leaf, panel, row_map, inv_parent):
    rows, cols = inv_leaf.shape[1:]
    pb = panel.shape[1]
    R = rhs_leaf.shape[2]
    own = rhs_parent.shape[0]
    n8, blk, H = rows // 8, pb // 4, R // 2
    prow, pcol = inv_parent.shape
    V = pltpu.VMEM
    any_spec = pl.BlockSpec(memory_space=pl.ANY)
    vmem = pl.BlockSpec(memory_space=pltpu.VMEM)
    scratch = [
        V((rows, cols), BF), V((pb, rows), BF), V((prow, pcol), BF), V((cols, R), BF), V((own, R), BF),
        V((4, n8, R), BF), V((4, n8, R), BF), V((4, n8, R), BF), V((n8, R), F32), V((6, n8 // 2, R), BF),
        V((4, 2, n8, R), BF), V((R, n8), BF),
        V((pb, R), F32), V((4, blk, R), BF), V((6, blk // 2, R), BF),
        V((32, 8, R), F32), V((32, 8, R), F32), V((32, 8, R), F32), V((32, 8, own), F32), V((32, 8, own), F32),
        V((4 * own, 256), BF), V((256, 4 * own), BF), V((256, blk), BF), V((blk, 256), BF),
        V((4, own, R), BF), V((6, own // 2, R), BF), V((2, 4, 4, 2, own, H), BF),
        V((4, own, R), BF), V((6, own // 2, R), BF), V((4, R, own), BF),
        V((2, 4, 4, H, own), BF), V((2, 4, 4, H, own), BF), V((2, 4, 4, H, own), BF), V((2, 4, 4, H, own), F32),
        V((6, 2, H, own), BF), V((6, H // 2, own), BF), V((6, 2, H, own), BF), V((6, H // 2, own), BF),
        V((4, own, R), BF), V((4, blk, R), BF),
        V((4, R, n8), BF), V((4, R, n8), BF), V((4, R, n8), BF), V((R, n8), F32), V((6, H, n8), BF),
        V((4, 2, R, n8), BF),
        V((4, R, n8), F32), V((4, R, n8), BF), V((6, H, n8), BF),
        pltpu.SemaphoreType.DMA((200,)), pltpu.SemaphoreType.DMA((200,)), pltpu.SemaphoreType.DMA((12,)),
        pltpu.SemaphoreType.DMA((3,)), pltpu.SemaphoreType.DMA((3,)),
    ]
    sol_leaf, sol_parent = pl.pallas_call(
        kernel,
        out_shape=(
            jax.ShapeDtypeStruct((4, n8, R), BF),
            jax.ShapeDtypeStruct((own, R), BF),
        ),
        in_specs=[any_spec] * 5 + [vmem],
        out_specs=(vmem, vmem),
        scratch_shapes=scratch,
        compiler_params=pltpu.CompilerParams(
            collective_id=0, has_side_effects=True, vmem_limit_bytes=60 * 1024 * 1024
        ),
    )(
        rhs_leaf[0],
        rhs_parent,
        inv_leaf[0],
        panel[0],
        inv_parent,
        row_map[0].reshape(4, blk),
    )
    return (sol_leaf.reshape(1, 4 * n8, R), sol_parent)


def solution(mesh):
    in_specs = (
        P("leaf", "col", None),
        P(("leaf", "row", "col"), None),
        P("leaf", "row", "col"),
        P("leaf", "col", "row"),
        P("leaf", "col"),
        P(("row", "col"), "leaf"),
    )
    out_specs = (P("leaf", "col", None), P(("leaf", "row", "col"), None))
    return jax.shard_map(
        per_device, mesh=mesh, in_specs=in_specs, out_specs=out_specs, check_vma=False
    )
```

```python
import jax
import jax.numpy as jnp
from jax import lax
from jax.experimental import pallas as pl
from jax.experimental.pallas import tpu as pltpu
from jax.sharding import PartitionSpec as P

MESH = pl.DeviceIdType.MESH
BF = jnp.bfloat16
F32 = jnp.float32


def dot(a, b):
    return jnp.dot(a, b, preferred_element_type=F32)


class Comm:
    def __init__(self, ssem, rsem):
        self.ssem, self.rsem, self.n, self.sent = ssem, rsem, 0, []
        self.l, self.r, self.c = (lax.axis_index(a) for a in ("leaf", "row", "col"))
        self.x, self.k = self.c // 2, self.c % 2

    def at(self, axis, delta):
        if axis == "x":
            return (self.l, self.r, ((self.x + delta + 4) % 4) * 2 + self.k)
        if axis == "z":
            return (self.l, (self.r + delta + 4) % 4, self.c)
        if axis == "y":
            return ((self.l + delta + 4) % 4, self.r, self.c)
        return (self.l, self.r, self.x * 2 + 1 - self.k)

    def make(self, src, dst, device):
        at = self.n
        self.n += 1
        return pltpu.make_async_remote_copy(
            src_ref=src,
            dst_ref=dst,
            send_sem=self.ssem.at[at],
            recv_sem=self.rsem.at[at],
            device_id=device,
            device_id_type=MESH,
        )

    def send(self, src, dst, axis, delta=0):
        copy = self.make(src, dst, self.at(axis, delta))
        copy.start()
        self.sent.append(copy)
        return copy

    def drain(self):
        for copy in self.sent:
            copy.wait_send()
        self.sent = []


class Sum:
    def __init__(self, comm, axis, q, slot):
        self.comm, self.axis, self.q, self.slot, self.copies = comm, axis, q, slot, {}

    def put(self, d):
        self.copies[d] = self.comm.send(self.q(d), self.slot(d - 1), self.axis, d)

    def run(self):
        for d in (2, 1, 3):
            self.put(d)

    def total(self, own):
        for d in (1, 3, 2):
            self.copies[d].wait_recv()
            own = own + self.slot(d - 1)[...].astype(F32)
        return own


class Gather:
    def __init__(self, comm, axis, me, g):
        self.me = me
        self.copies = {d: comm.send(g(me), g(me), axis, d) for d in (2, 1, 3)}

    def wait(self, d):
        self.copies[d].wait_recv()
        return (self.me + 4 - d) % 4

    def run(self):
        for d in (1, 3, 2):
            self.wait(d)


def kernel(
    x_hbm, rp_hbm, a_hbm, b_hbm, p_hbm, rm_ref,
    out_ref, solp_ref,
    a_v, b_v, p_v, x_v, rp_v,
    sb1, rb1, q1, own1, rr1, y_v, yt,
    u_acc, g32, g_v, r1_v, r2_v, qs, qr, t1, t1t, s1, s1t,
    q3, rr3, gred, q4, rr4, ft,
    sb5, rb5, q5, own5, rz0, rx0, rx1, rz1,
    sp, sb7, rb7, q7, own7, rr7, ct,
    acc8, q8, rr8,
    ssem, rsem, lsem, asem, bsem,
):
    cm = Comm(ssem, rsem)
    l, r, c, x, k = cm.l, cm.r, cm.c, cm.x, cm.k
    me = r * 8 + c
    n8 = y_v.shape[2]
    R = x_v.shape[1]
    H = R // 2
    own = rp_v.shape[0]
    blk = s1t.shape[1]

    loads = [pltpu.make_async_copy(x_hbm, x_v, lsem.at[0])]
    for i, d in enumerate((2, 3, 1, 0)):
        for j, core in enumerate((1 - k, k)):
            rows = pl.ds(pl.multiple_of((((x + d) % 4) * 2 + core) * n8, n8), n8)
            loads.append(pltpu.make_async_copy(a_hbm.at[rows], a_v.at[rows], lsem.at[1 + 2 * i + j]))
    loads.append(pltpu.make_async_copy(rp_hbm, rp_v, lsem.at[9]))
    loads.append(pltpu.make_async_copy(b_hbm, b_v, lsem.at[10]))
    loads.append(pltpu.make_async_copy(p_hbm, p_v, lsem.at[11]))
    for load in loads:
        load.start()

    barrier = pltpu.get_barrier_semaphore()

    def greet(n, _):
        to = (me + n) % 32
        pl.semaphore_signal(barrier, inc=1, device_id=(l, to // 8, to % 8), device_id_type=MESH)
        return 0

    lax.fori_loop(1, 32, greet, 0)
    for d in (1, 2, 3):
        pl.semaphore_signal(barrier, inc=1, device_id=((l + d) % 4, r, c), device_id_type=MESH)

    def a_rows(d, core):
        return pl.ds(pl.multiple_of((((x + d) % 4) * 2 + core) * n8, n8), n8)

    sib = {}
    loads[0].wait()
    xv = x_v[...]
    ring = Sum(cm, "x", lambda d: q1.at[d], lambda i: rr1.at[i])
    for i, d in enumerate((2, 3, 1, 0)):
        loads[1 + 2 * i].wait()
        sb1[d] = dot(a_v[a_rows(d, 1 - k), :], xv).astype(BF)
        if i == 0:
            pl.semaphore_wait(barrier, 34)
        sib[d] = cm.send(sb1.at[d], rb1.at[d], "c")
    for i, d in enumerate((2, 3, 1, 0)):
        loads[2 + 2 * i].wait()
        part = dot(a_v[a_rows(d, k), :], xv)
        sib[d].wait_recv()
        part = part + rb1[d].astype(F32)
        if d:
            q1[d] = part.astype(BF)
            ring.put(d)
        else:
            own1[...] = part

    shift = own.bit_length() - 1
    before = lax.broadcasted_iota(jnp.int32, (blk, blk), 0) < lax.broadcasted_iota(jnp.int32, (blk, blk), 1)
    for i in range(4):
        e = rm_ref[i : i + 1, :]
        owner = lax.shift_right_logical(e, shift)
        local = lax.bitwise_and(e, own - 1).astype(F32)
        across = jnp.broadcast_to(owner.astype(F32), (blk, blk))
        rank = jnp.sum(jnp.where((across == across.T) & before, 1.0, 0.0), axis=0, keepdims=True)
        place = lax.bitwise_and(owner, 31) * 8 + lax.shift_right_logical(owner, 5) * 2
        place = place.astype(F32) + rank
        pick = jnp.where(
            lax.broadcasted_iota(jnp.int32, (256, blk), 0).astype(F32) == jnp.broadcast_to(place, (256, blk)), 1.0, 0.0
        )
        s1[i] = pick.astype(BF)
        near = (lax.broadcasted_iota(jnp.int32, (64, blk), 0) + r * 64).astype(F32)
        where = jnp.where(near == jnp.broadcast_to(place, (64, blk)), jnp.broadcast_to(local + 1.0, (64, blk)), 0.0)
        qv = jnp.sum(where, axis=1, keepdims=True)
        qs[:, i * 8 : (i + 1) * 8, :] = jnp.broadcast_to(qv, (64, own)).reshape(8, 8, own)
    qr[pl.ds(c, 1)] = qs[pl.ds(c, 1)]

    def row_copy(n):
        to = (c + n) % 8
        return pltpu.make_async_remote_copy(
            src_ref=qs.at[to], dst_ref=qr.at[c], send_sem=asem.at[0], recv_sem=bsem.at[0],
            device_id=(l, r, to), device_id_type=MESH,
        )

    for n in range(1, 8):
        row_copy(n).start()

    tot = ring.total(own1[...])
    y_v[x, k] = tot.astype(BF)

    gat = Gather(cm, "x", x, lambda i: y_v.at[i, k])
    fwd = {0: cm.send(y_v.at[x, k], y_v.at[x, k], "c")}
    yt[...] = tot.T.astype(BF)
    loads[10].wait()

    def panel_cols(xx, core):
        return pl.ds(pl.multiple_of((xx * 2 + core) * n8, n8), n8)

    def push(xx, core, first=False):
        part = dot(b_v[:, panel_cols(xx, core)], y_v[xx, core])
        u_acc[...] = part if first else u_acc[...] + part

    push(x, k, True)
    fwd[0].wait_recv()
    push(x, 1 - k)
    at = {}
    for d in (1, 3, 2):
        at[d] = gat.wait(d)
        fwd[d] = cm.send(y_v.at[at[d], k], y_v.at[at[d], k], "c")
        push(at[d], k)
        if d != 1:
            last = 1 if d == 3 else 3
            fwd[last].wait_recv()
            push(at[last], 1 - k)
    fwd[2].wait_recv()
    push(at[2], 1 - k)

    def plane_exchange(src, src_at, dst, which):
        def one(n, _):
            to = (me + n) % 32
            pltpu.make_async_remote_copy(
                src_ref=src.at[src_at(to)], dst_ref=dst.at[me], send_sem=asem.at[which], recv_sem=bsem.at[which],
                device_id=(l, to // 8, to % 8), device_id_type=MESH,
            ).start()
            return 0

        lax.fori_loop(1, 32, one, 0)

    def plane_wait(dst, which):
        copy = pltpu.make_async_remote_copy(
            src_ref=dst.at[pl.ds(0, 31)], dst_ref=dst.at[pl.ds(0, 31)], send_sem=asem.at[which],
            recv_sem=bsem.at[which], device_id=cm.at("c", 0), device_id_type=MESH,
        )
        copy.wait_send()
        copy.wait_recv()

    for i in range(4):
        rows = u_acc[i * blk : (i + 1) * blk].astype(BF)
        g32[:, i * 8 : (i + 1) * 8, :] = dot(s1[i], rows).reshape(32, 8, R)
    g_v[...] = g32[...].astype(BF)
    plane_exchange(g_v, lambda to: to, r1_v, 1)
    r1_v[pl.ds(me, 1)] = g_v[pl.ds(me, 1)]

    copy = pltpu.make_async_remote_copy(
        src_ref=qs.at[pl.ds(0, 7)], dst_ref=qr.at[pl.ds(0, 7)], send_sem=asem.at[0], recv_sem=bsem.at[0],
        device_id=cm.at("c", 0), device_id_type=MESH,
    )
    copy.wait_send()
    copy.wait_recv()
    seen = qr[...].reshape(256, own)
    lane = lax.broadcasted_iota(jnp.int32, (256, own), 1).astype(F32) + 1.0
    leaf_of = lax.bitwise_and(
        lax.shift_right_logical(lax.broadcasted_iota(jnp.int32, (256, own), 0), 1), 3
    )
    for i in range(4):
        table = jnp.where((seen == lane) & (leaf_of == i), 1.0, 0.0)
        t1t[:, i * own : (i + 1) * own] = table.astype(BF)
        t1[i * own : (i + 1) * own, :] = table.T.astype(BF)

    plane_wait(r1_v, 1)
    got = r1_v[0:8].astype(F32)
    for i in range(1, 4):
        got = got + r1_v[8 * i : 8 * i + 8].astype(F32)
    got = got.reshape(256, R).astype(BF)

    def t_rows(d):
        return t1[pl.ds(pl.multiple_of(((l + d) % 4) * own, own), own), :]

    ring = Sum(cm, "y", lambda d: q3.at[d], lambda i: rr3.at[i])
    for d in (2, 1, 3):
        q3[d] = dot(t_rows(d), got).astype(BF)
        ring.put(d)
    tot = dot(t_rows(0), got)
    loads[9].wait()
    tot = rp_v[...].astype(F32) - ring.total(tot)
    for h in range(2):
        gred[h, r, x, k] = tot[:, h * H : (h + 1) * H].astype(BF)

    g0 = Gather(cm, "x", x, lambda i: gred.at[0, r, i, k])
    g1 = Gather(cm, "z", r, lambda i: gred.at[1, i, x, k])
    for i in range(4):
        s1t[i] = s1[i].astype(F32).T.astype(BF)
    g0.run()
    g2 = Gather(cm, "z", r, lambda i: gred.at[0, i, :, k])
    g1.run()
    g3 = Gather(cm, "x", x, lambda i: gred.at[1, :, i, k])
    fwd = [cm.send(gred.at[0, r, :, k], gred.at[0, r, :, k], "c")]
    fwd.append(cm.send(gred.at[1, :, x, k], gred.at[1, :, x, k], "c"))
    loads[11].wait()
    for d in (1, 3, 2):
        i = g2.wait(d)
        fwd.append(cm.send(gred.at[0, i, :, k], gred.at[0, i, :, k], "c"))
        i = g3.wait(d)
        fwd.append(cm.send(gred.at[1, :, i, k], gred.at[1, :, i, k], "c"))
    for copy in fwd:
        copy.wait_recv()

    parent = None
    for i in range(4):
        rhs = jnp.concatenate([gred[h, i].reshape(8 * own, H) for h in range(2)], axis=1)
        part = dot(p_v[:, i * 8 * own : (i + 1) * 8 * own], rhs)
        parent = part if parent is None else parent + part
    u_acc[: 4 * own] = parent

    def f_rows(d):
        return u_acc[pl.ds(pl.multiple_of(((l + d) % 4) * own, own), own), :]

    ring = Sum(cm, "y", lambda d: q4.at[d], lambda i: rr4.at[i])
    for d in (2, 1, 3):
        q4[d] = f_rows(d).astype(BF)
        ring.put(d)
    ft[l] = ring.total(f_rows(0)).T.astype(BF)
    Gather(cm, "y", l, lambda i: ft.at[i]).run()

    lhs = jnp.concatenate([ft[i] for i in range(4)], axis=1)
    sib = {}
    for dr in (2, 3, 1, 0):
        for dx in range(4):
            block = ((r + dr) % 4) * 4 + (x + dx) % 4
            part = dot(lhs, p_v[:, pl.ds(pl.multiple_of(block * 2 * own, 2 * own), 2 * own)])
            lo, hi = part[:, :own], part[:, own:]
            mine = jnp.where(k == 0, lo, hi)
            sib_part = jnp.where(k == 0, hi, lo).astype(BF)
            for h in range(2):
                own5[h, dr, dx] = mine[h * H : (h + 1) * H]
                sb5[h, dr, dx] = sib_part[h * H : (h + 1) * H]
        sib[dr] = cm.send(sb5.at[:, dr], rb5.at[:, dr], "c")
    z0 = Sum(cm, "z", lambda d: q5.at[0, d], lambda i: rz0.at[i])
    x1 = Sum(cm, "x", lambda d: q5.at[1, :, d], lambda i: rx1.at[i])
    for dr in (2, 3, 1, 0):
        sib[dr].wait_recv()
        own5[:, dr] = own5[:, dr] + rb5[:, dr].astype(F32)
        q5[:, dr] = own5[:, dr].astype(BF)
        if dr:
            z0.put(dr)
    x1.run()
    tot0 = z0.total(own5[0, 0])
    q5[0, 0] = tot0.astype(BF)
    x0 = Sum(cm, "x", lambda d: q5.at[0, 0, d], lambda i: rx0.at[i])
    x0.run()
    tot1 = x1.total(own5[1, :, 0])
    q5[1, :, 0] = tot1.astype(BF)
    z1 = Sum(cm, "z", lambda d: q5.at[1, d, 0], lambda i: rz1.at[i])
    z1.run()
    lo = x0.total(tot0[0])
    hi = z1.total(tot1[0])
    solved = jnp.concatenate([lo, hi], axis=0).T.astype(BF)
    sp[l] = solved

    gat = Gather(cm, "y", l, lambda i: sp.at[i])
    solp_ref[...] = solved
    gat.run()
    g8 = dot(t1t[...], sp[...].reshape(4 * own, R)).astype(BF).reshape(8, 32, R)
    g_v[0:8] = g8
    plane_exchange(g_v, lambda to: to % 8, r2_v, 2)
    r2_v[pl.ds(me, 1)] = g_v[pl.ds(c, 1)]
    plane_wait(r2_v, 2)
    g32[...] = r2_v[...].astype(F32)
    picked = jnp.concatenate(
        [dot(s1t[i], g32[:, i * 8 : (i + 1) * 8, :].reshape(256, R).astype(BF)) for i in range(4)], axis=0
    )
    picked = picked.T.astype(BF)

    sib = {}
    ring = Sum(cm, "x", lambda d: q7.at[d], lambda i: rr7.at[i])
    for d in (2, 3, 1, 0):
        sb7[d] = dot(picked, b_v[:, panel_cols((x + d) % 4, 1 - k)]).astype(BF)
        sib[d] = cm.send(sb7.at[d], rb7.at[d], "c")
    for d in (2, 3, 1, 0):
        part = dot(picked, b_v[:, panel_cols((x + d) % 4, k)])
        sib[d].wait_recv()
        part = part + rb7[d].astype(F32)
        if d:
            q7[d] = part.astype(BF)
            ring.put(d)
        else:
            own7[...] = part
    tot = ring.total(own7[...])
    ct[x, k] = (yt[...].astype(F32) - tot).astype(BF)

    gat = Gather(cm, "x", x, lambda i: ct.at[i, k])
    fwd = {0: cm.send(ct.at[x, k], ct.at[x, k], "c")}
    ring = Sum(cm, "z", lambda d: q8.at[d], lambda i: rr8.at[i])

    def pull(xx, core, first=False, last=False):
        lhs = ct[xx, core]
        rows = pl.ds(pl.multiple_of((xx * 2 + core) * n8, n8), n8)
        for d in (2, 1, 3, 0):
            cols = pl.ds(pl.multiple_of(((r + d) % 4) * n8, n8), n8)
            part = dot(lhs, a_v[rows, cols])
            part = part if first else acc8[d] + part
            if last and d:
                q8[d] = part.astype(BF)
                ring.put(d)
            else:
                acc8[d] = part

    pull(x, k, True)
    fwd[0].wait_recv()
    pull(x, 1 - k)
    at = {}
    for d in (1, 3, 2):
        at[d] = gat.wait(d)
        fwd[d] = cm.send(ct.at[at[d], k], ct.at[at[d], k], "c")
        pull(at[d], k)
        if d != 1:
            last = 1 if d == 3 else 3
            fwd[last].wait_recv()
            pull(at[last], 1 - k)
    fwd[2].wait_recv()
    pull(at[2], 1 - k, last=True)
    out_ref[r] = ring.total(acc8[0]).T.astype(BF)
    Gather(cm, "z", r, lambda i: out_ref.at[i]).run()
    cm.drain()


def per_device(rhs_leaf, rhs_parent, inv_leaf, panel, row_map, inv_parent):
    rows, cols = inv_leaf.shape[1:]
    pb = panel.shape[1]
    R = rhs_leaf.shape[2]
    own = rhs_parent.shape[0]
    n8, blk, H = rows // 8, pb // 4, R // 2
    prow, pcol = inv_parent.shape
    V = pltpu.VMEM
    any_spec = pl.BlockSpec(memory_space=pl.ANY)
    vmem = pl.BlockSpec(memory_space=pltpu.VMEM)
    scratch = [
        V((rows, cols), BF), V((pb, rows), BF), V((prow, pcol), BF), V((cols, R), BF), V((own, R), BF),
        V((4, n8, R), BF), V((4, n8, R), BF), V((4, n8, R), BF), V((n8, R), F32), V((3, n8, R), BF),
        V((4, 2, n8, R), BF), V((R, n8), BF),
        V((pb, R), F32), V((32, 32, R), F32), V((32, 32, R), BF), V((32, 32, R), BF), V((32, 32, R), BF),
        V((8, 32, own), F32), V((8, 32, own), F32),
        V((4 * own, 256), BF), V((256, 4 * own), BF), V((4, 256, blk), BF), V((4, blk, 256), BF),
        V((4, own, R), BF), V((3, own, R), BF), V((2, 4, 4, 2, own, H), BF),
        V((4, own, R), BF), V((3, own, R), BF), V((4, R, own), BF),
        V((2, 4, 4, H, own), BF), V((2, 4, 4, H, own), BF), V((2, 4, 4, H, own), BF), V((2, 4, 4, H, own), F32),
        V((3, 4, H, own), BF), V((3, H, own), BF), V((3, 4, H, own), BF), V((3, H, own), BF),
        V((4, own, R), BF),
        V((4, R, n8), BF), V((4, R, n8), BF), V((4, R, n8), BF), V((R, n8), F32), V((3, R, n8), BF),
        V((4, 2, R, n8), BF),
        V((4, R, n8), F32), V((4, R, n8), BF), V((3, R, n8), BF),
        pltpu.SemaphoreType.DMA((100,)), pltpu.SemaphoreType.DMA((100,)), pltpu.SemaphoreType.DMA((12,)),
        pltpu.SemaphoreType.DMA((3,)), pltpu.SemaphoreType.DMA((3,)),
    ]
    sol_leaf, sol_parent = pl.pallas_call(
        kernel,
        out_shape=(
            jax.ShapeDtypeStruct((4, n8, R), BF),
            jax.ShapeDtypeStruct((own, R), BF),
        ),
        in_specs=[any_spec] * 5 + [vmem],
        out_specs=(vmem, vmem),
        scratch_shapes=scratch,
        compiler_params=pltpu.CompilerParams(
            collective_id=0, has_side_effects=True, vmem_limit_bytes=60 * 1024 * 1024
        ),
    )(
        rhs_leaf[0],
        rhs_parent,
        inv_leaf[0],
        panel[0],
        inv_parent,
        row_map[0].reshape(4, blk),
    )
    return (sol_leaf.reshape(1, 4 * n8, R), sol_parent)


def solution(mesh):
    in_specs = (
        P("leaf", "col", None),
        P(("leaf", "row", "col"), None),
        P("leaf", "row", "col"),
        P("leaf", "col", "row"),
        P("leaf", "col"),
        P(("row", "col"), "leaf"),
    )
    out_specs = (P("leaf", "col", None), P(("leaf", "row", "col"), None))
    return jax.shard_map(
        per_device, mesh=mesh, in_specs=in_specs, out_specs=out_specs, check_vma=False
    )
```

```python
import jax
import jax.numpy as jnp
from jax import lax
from jax.experimental import pallas as pl
from jax.experimental.pallas import tpu as pltpu
from jax.sharding import PartitionSpec as P

MESH = pl.DeviceIdType.MESH
BF = jnp.bfloat16
F32 = jnp.float32


def dot(a, b):
    return jnp.dot(a, b, preferred_element_type=F32)


class Comm:
    def __init__(self, ssem, rsem):
        self.ssem, self.rsem, self.n, self.sent = ssem, rsem, 0, []
        self.l, self.r, self.c = (lax.axis_index(a) for a in ("leaf", "row", "col"))
        self.x, self.k = self.c // 2, self.c % 2

    def at(self, axis, delta):
        if axis == "x":
            return (self.l, self.r, ((self.x + delta + 4) % 4) * 2 + self.k)
        if axis == "z":
            return (self.l, (self.r + delta + 4) % 4, self.c)
        if axis == "y":
            return ((self.l + delta + 4) % 4, self.r, self.c)
        return (self.l, self.r, self.x * 2 + 1 - self.k)

    def make(self, src, dst, device):
        at = self.n
        self.n += 1
        return pltpu.make_async_remote_copy(
            src_ref=src,
            dst_ref=dst,
            send_sem=self.ssem.at[at],
            recv_sem=self.rsem.at[at],
            device_id=device,
            device_id_type=MESH,
        )

    def send(self, src, dst, axis, delta=0):
        copy = self.make(src, dst, self.at(axis, delta))
        copy.start()
        self.sent.append(copy)
        return copy

    def drain(self):
        for copy in self.sent:
            copy.wait_send()
        self.sent = []


class Sum:
    def __init__(self, comm, axis, q, slot):
        self.comm, self.axis, self.q, self.slot, self.copies = comm, axis, q, slot, {}

    def put(self, d):
        self.copies[d] = self.comm.send(self.q(d), self.slot(d - 1), self.axis, d)

    def run(self):
        for d in (2, 1, 3):
            self.put(d)

    def total(self, own):
        for d in (1, 3, 2):
            self.copies[d].wait_recv()
            own = own + self.slot(d - 1)[...].astype(F32)
        return own


class Gather:
    def __init__(self, comm, axis, me, g):
        self.me = me
        self.copies = {d: comm.send(g(me), g(me), axis, d) for d in (2, 1, 3)}

    def wait(self, d):
        self.copies[d].wait_recv()
        return (self.me + 4 - d) % 4

    def run(self):
        for d in (1, 3, 2):
            self.wait(d)


def kernel(
    x_hbm, rp_hbm, a_hbm, b_hbm, p_hbm, rm_ref,
    out_ref, solp_ref,
    a_v, b_v, p_v, x_v, rp_v,
    sb1_, rb1_, q1_, own1_, rr1_, y_, yt_,
    u_acc_, g32_, g_, r1_, r2_, qs, qr, t1, t1t, s1, s1t,
    q3_, rr3_, gred_, q4_, rr4_, ft_,
    sb5_, rb5_, q5_, own5_, ra5_, rb5b_,
    sp_, sb7_, rb7_, q7_, own7_, rr7_, ct_,
    acc8_, q8_, rr8_,
    ssem, rsem, lsem, asem, bsem,
):
    cm = Comm(ssem, rsem)
    l, r, c, x, k = cm.l, cm.r, cm.c, cm.x, cm.k
    me = r * 8 + c
    n8 = y_.shape[3]
    W = x_v.shape[1] // 2
    own = rp_v.shape[0]
    blk = s1t.shape[1]
    order = ((1, 2), (1, 3), (0, 2), (1, 1), (0, 3), (1, 0), (0, 1), (0, 0))

    def a_rows(d, away):
        core = 1 - k if away else k
        return pl.ds(pl.multiple_of((((x + d) % 4) * 2 + core) * n8, n8), n8)

    loads = [pltpu.make_async_copy(x_hbm, x_v, lsem.at[0])]
    for i, (away, d) in enumerate(order):
        rows = a_rows(d, away)
        loads.append(pltpu.make_async_copy(a_hbm.at[rows], a_v.at[rows], lsem.at[1 + i]))
    loads.append(pltpu.make_async_copy(rp_hbm, rp_v, lsem.at[9]))
    loads.append(pltpu.make_async_copy(b_hbm, b_v, lsem.at[10]))
    loads.append(pltpu.make_async_copy(p_hbm, p_v, lsem.at[11]))
    for load in loads:
        load.start()
    loaded = set()

    def need(i):
        if i not in loaded:
            loaded.add(i)
            loads[i].wait()

    barrier = pltpu.get_barrier_semaphore()

    def greet(n, _):
        to = (me + n) % 32
        pl.semaphore_signal(barrier, inc=1, device_id=(l, to // 8, to % 8), device_id_type=MESH)
        return 0

    lax.fori_loop(1, 32, greet, 0)
    for d in (1, 2, 3):
        pl.semaphore_signal(barrier, inc=1, device_id=((l + d) % 4, r, c), device_id_type=MESH)

    def panel_cols(xx, core):
        return pl.ds(pl.multiple_of((xx * 2 + core) * n8, n8), n8)

    def row_wait():
        copy = pltpu.make_async_remote_copy(
            src_ref=qs.at[pl.ds(0, 7)], dst_ref=qr.at[pl.ds(0, 7)], send_sem=asem.at[0], recv_sem=bsem.at[0],
            device_id=cm.at("c", 0), device_id_type=MESH,
        )
        copy.wait_send()
        copy.wait_recv()

    def plane_exchange(src, src_at, dst, which):
        def one(n, _):
            to = (me + n) % 32
            pltpu.make_async_remote_copy(
                src_ref=src.at[src_at(to)], dst_ref=dst.at[me], send_sem=asem.at[which], recv_sem=bsem.at[which],
                device_id=(l, to // 8, to % 8), device_id_type=MESH,
            ).start()
            return 0

        lax.fori_loop(1, 32, one, 0)

    def plane_wait(dst, which):
        copy = pltpu.make_async_remote_copy(
            src_ref=dst.at[pl.ds(0, 31)], dst_ref=dst.at[pl.ds(0, 31)], send_sem=asem.at[which],
            recv_sem=bsem.at[which], device_id=cm.at("c", 0), device_id_type=MESH,
        )
        copy.wait_send()
        copy.wait_recv()

    def slot_tables():
        shift = own.bit_length() - 1
        before = lax.broadcasted_iota(jnp.int32, (blk, blk), 0) < lax.broadcasted_iota(jnp.int32, (blk, blk), 1)
        for i in range(4):
            e = rm_ref[i : i + 1, :]
            owner = lax.shift_right_logical(e, shift)
            local = lax.bitwise_and(e, own - 1).astype(F32)
            across = jnp.broadcast_to(owner.astype(F32), (blk, blk))
            rank = jnp.sum(jnp.where((across == across.T) & before, 1.0, 0.0), axis=0, keepdims=True)
            place = lax.bitwise_and(owner, 31) * 8 + lax.shift_right_logical(owner, 5) * 2
            place = place.astype(F32) + rank
            pick = jnp.where(
                lax.broadcasted_iota(jnp.int32, (256, blk), 0).astype(F32) == jnp.broadcast_to(place, (256, blk)),
                1.0,
                0.0,
            )
            s1[i] = pick.astype(BF)
            near = (lax.broadcasted_iota(jnp.int32, (64, blk), 0) + r * 64).astype(F32)
            where = jnp.where(near == jnp.broadcast_to(place, (64, blk)), jnp.broadcast_to(local + 1.0, (64, blk)), 0.0)
            qv = jnp.sum(where, axis=1, keepdims=True)
            qs[:, i * 8 : (i + 1) * 8, :] = jnp.broadcast_to(qv, (64, own)).reshape(8, 8, own)
        qr[pl.ds(c, 1)] = qs[pl.ds(c, 1)]
        for n in range(1, 8):
            to = (c + n) % 8
            pltpu.make_async_remote_copy(
                src_ref=qs.at[to], dst_ref=qr.at[c], send_sem=asem.at[0], recv_sem=bsem.at[0],
                device_id=(l, r, to), device_id_type=MESH,
            ).start()

    def parent_tables():
        row_wait()
        seen = qr[...].reshape(256, own)
        lane = lax.broadcasted_iota(jnp.int32, (256, own), 1).astype(F32) + 1.0
        leaf_of = lax.bitwise_and(
            lax.shift_right_logical(lax.broadcasted_iota(jnp.int32, (256, own), 0), 1), 3
        )
        for i in range(4):
            table = jnp.where((seen == lane) & (leaf_of == i), 1.0, 0.0)
            t1t[:, i * own : (i + 1) * own] = table.astype(BF)
            t1[i * own : (i + 1) * own, :] = table.T.astype(BF)

    def chain(hf):
        sb1, rb1, q1, own1, rr1, y_v, yt = (v.at[hf] for v in (sb1_, rb1_, q1_, own1_, rr1_, y_, yt_))
        u_acc, g32, g_v, r1_v, r2_v = (v.at[hf] for v in (u_acc_, g32_, g_, r1_, r2_))
        q3, rr3, gred, q4, rr4, ft = (v.at[hf] for v in (q3_, rr3_, gred_, q4_, rr4_, ft_))
        sb5, rb5, q5, own5, ra5, rb5b = (v.at[hf] for v in (sb5_, rb5_, q5_, own5_, ra5_, rb5b_))
        sp, sb7, rb7, q7, own7, rr7, ct = (v.at[hf] for v in (sp_, sb7_, rb7_, q7_, own7_, rr7_, ct_))
        acc8, q8, rr8 = (v.at[hf] for v in (acc8_, q8_, rr8_))
        cols = pl.ds(hf * W, W)

        sib = {}
        need(0)
        xv = x_v[:, hf * W : (hf + 1) * W]
        ring = Sum(cm, "x", lambda d: q1.at[d], lambda i: rr1.at[i])
        for i, (away, d) in enumerate(order):
            need(1 + i)
            part = dot(a_v[a_rows(d, away), :], xv)
            if away:
                sb1[d] = part.astype(BF)
                if hf == 0 and i == 0:
                    pl.semaphore_wait(barrier, 34)
                sib[d] = cm.send(sb1.at[d], rb1.at[d], "c")
                continue
            sib[d].wait_recv()
            part = part + rb1[d].astype(F32)
            if d:
                q1[d] = part.astype(BF)
                ring.put(d)
            else:
                own1[...] = part
        yield
        if hf == 0:
            slot_tables()
        tot = ring.total(own1[...])
        y_v[x, k] = tot.astype(BF)

        fwd = {0: cm.send(y_v.at[x, k], y_v.at[x, k], "c")}
        gat = Gather(cm, "x", x, lambda i: y_v.at[i, k])
        yt[...] = tot.T.astype(BF)
        need(10)

        def push(xx, core, first=False):
            part = dot(b_v[:, panel_cols(xx, core)], y_v[xx, core])
            u_acc[...] = part if first else u_acc[...] + part

        push(x, k, True)
        yield
        fwd[0].wait_recv()
        push(x, 1 - k)
        yield
        at = {}
        for d in (1, 3, 2):
            at[d] = gat.wait(d)
            fwd[d] = cm.send(y_v.at[at[d], k], y_v.at[at[d], k], "c")
            push(at[d], k)
            if d == 1:
                continue
            last = 1 if d == 3 else 3
            fwd[last].wait_recv()
            push(at[last], 1 - k)
            yield
        fwd[2].wait_recv()
        push(at[2], 1 - k)

        for i in range(4):
            rows = u_acc[i * blk : (i + 1) * blk].astype(BF)
            g32[:, i * 8 : (i + 1) * 8, :] = dot(s1[i], rows).reshape(32, 8, W)
        g_v[...] = g32[...].astype(BF)
        plane_exchange(g_v, lambda to: to, r1_v, 1 + 2 * hf)
        r1_v[pl.ds(me, 1)] = g_v[pl.ds(me, 1)]
        yield
        if hf == 0:
            parent_tables()
        plane_wait(r1_v, 1 + 2 * hf)
        got = r1_v[0:8].astype(F32)
        for i in range(1, 4):
            got = got + r1_v[8 * i : 8 * i + 8].astype(F32)
        got = got.reshape(256, W).astype(BF)

        def t_rows(d):
            return t1[pl.ds(pl.multiple_of(((l + d) % 4) * own, own), own), :]

        ring = Sum(cm, "y", lambda d: q3.at[d], lambda i: rr3.at[i])
        for d in (2, 1, 3):
            q3[d] = dot(t_rows(d), got).astype(BF)
            ring.put(d)
        tot = dot(t_rows(0), got)
        yield
        need(9)
        tot = rp_v[:, hf * W : (hf + 1) * W].astype(F32) - ring.total(tot)
        gred[r, x, k] = tot.astype(BF)

        if hf == 0:
            gat = Gather(cm, "x", x, lambda i: gred.at[r, i, k])
        else:
            gat = Gather(cm, "z", r, lambda i: gred.at[i, x, k])
            for i in range(4):
                s1t[i] = s1[i].astype(F32).T.astype(BF)
        yield
        gat.run()
        if hf == 0:
            part = lambda i: gred.at[i, :, k]
            gat = Gather(cm, "z", r, part)
            mine = r
        else:
            part = lambda i: gred.at[:, i, k]
            gat = Gather(cm, "x", x, part)
            mine = x
        fwd = [cm.send(part(mine), part(mine), "c")]
        need(11)
        yield
        for d in (1, 3, 2):
            i = gat.wait(d)
            fwd.append(cm.send(part(i), part(i), "c"))
        yield
        for copy in fwd:
            copy.wait_recv()
        parent = dot(p_v[...], gred[...].reshape(32 * own, W))
        u_acc[: 4 * own] = parent

        def f_rows(d):
            return u_acc[pl.ds(pl.multiple_of(((l + d) % 4) * own, own), own), :]

        ring = Sum(cm, "y", lambda d: q4.at[d], lambda i: rr4.at[i])
        for d in (2, 1, 3):
            q4[d] = f_rows(d).astype(BF)
            ring.put(d)
        yield
        ft[l] = ring.total(f_rows(0)).T.astype(BF)
        gat = Gather(cm, "y", l, lambda i: ft.at[i])
        yield
        gat.run()

        lhs = jnp.concatenate([ft[i] for i in range(4)], axis=1)
        sib = {}
        for dr in (2, 3, 1, 0):
            for dx in range(4):
                block = ((r + dr) % 4) * 4 + (x + dx) % 4
                part = dot(lhs, p_v[:, pl.ds(pl.multiple_of(block * 2 * own, 2 * own), 2 * own)])
                lo, hi = part[:, :own], part[:, own:]
                own5[dr, dx] = jnp.where(k == 0, lo, hi)
                sb5[dr, dx] = jnp.where(k == 0, hi, lo).astype(BF)
            sib[dr] = cm.send(sb5.at[dr], rb5.at[dr], "c")
        yield
        if hf == 0:
            ring = Sum(cm, "z", lambda d: q5.at[d], lambda i: ra5.at[i])
        else:
            ring = Sum(cm, "x", lambda d: q5.at[:, d], lambda i: ra5.at[i])
        for dr in (2, 3, 1, 0):
            sib[dr].wait_recv()
            tot = own5[dr] + rb5[dr].astype(F32)
            own5[dr] = tot
            q5[dr] = tot.astype(BF)
            if dr and hf == 0:
                ring.put(dr)
        if hf == 1:
            ring.run()
        yield
        if hf == 0:
            tot = ring.total(own5[0])
            q5[0] = tot.astype(BF)
            ring = Sum(cm, "x", lambda d: q5.at[0, d], lambda i: rb5b.at[i])
        else:
            tot = ring.total(own5[:, 0])
            q5[:, 0] = tot.astype(BF)
            ring = Sum(cm, "z", lambda d: q5.at[d, 0], lambda i: rb5b.at[i])
        ring.run()
        yield
        solved = ring.total(tot[0]).T.astype(BF)
        sp[l] = solved

        gat = Gather(cm, "y", l, lambda i: sp.at[i])
        solp_ref[:, hf * W : (hf + 1) * W] = solved
        yield
        gat.run()
        g_v[0:8] = dot(t1t[...], sp[...].reshape(4 * own, W)).astype(BF).reshape(8, 32, W)
        plane_exchange(g_v, lambda to: to % 8, r2_v, 2 + 2 * hf)
        r2_v[pl.ds(me, 1)] = g_v[pl.ds(c, 1)]
        yield
        plane_wait(r2_v, 2 + 2 * hf)
        g32[...] = r2_v[...].astype(F32)
        picked = jnp.concatenate(
            [dot(s1t[i], g32[:, i * 8 : (i + 1) * 8, :].reshape(256, W).astype(BF)) for i in range(4)], axis=0
        )
        picked = picked.T.astype(BF)

        sib = {}
        ring = Sum(cm, "x", lambda d: q7.at[d], lambda i: rr7.at[i])
        for away, d in order:
            part = dot(picked, b_v[:, panel_cols((x + d) % 4, 1 - k if away else k)])
            if away:
                sb7[d] = part.astype(BF)
                sib[d] = cm.send(sb7.at[d], rb7.at[d], "c")
                continue
            sib[d].wait_recv()
            part = part + rb7[d].astype(F32)
            if d:
                q7[d] = part.astype(BF)
                ring.put(d)
            else:
                own7[...] = part
        yield
        tot = ring.total(own7[...])
        ct[x, k] = (yt[...].astype(F32) - tot).astype(BF)

        fwd = {0: cm.send(ct.at[x, k], ct.at[x, k], "c")}
        gat = Gather(cm, "x", x, lambda i: ct.at[i, k])
        ring = Sum(cm, "z", lambda d: q8.at[d], lambda i: rr8.at[i])

        def pull(xx, core, first=False, last=False):
            lhs = ct[xx, core]
            rows = pl.ds(pl.multiple_of((xx * 2 + core) * n8, n8), n8)
            for d in (2, 1, 3, 0):
                part = dot(lhs, a_v[rows, pl.ds(pl.multiple_of(((r + d) % 4) * n8, n8), n8)])
                part = part if first else acc8[d] + part
                if last and d:
                    q8[d] = part.astype(BF)
                    ring.put(d)
                else:
                    acc8[d] = part

        pull(x, k, True)
        yield
        fwd[0].wait_recv()
        pull(x, 1 - k)
        yield
        at = {}
        for d in (1, 3, 2):
            at[d] = gat.wait(d)
            fwd[d] = cm.send(ct.at[at[d], k], ct.at[at[d], k], "c")
            pull(at[d], k)
            if d == 1:
                continue
            last = 1 if d == 3 else 3
            fwd[last].wait_recv()
            pull(at[last], 1 - k)
            yield
        fwd[2].wait_recv()
        pull(at[2], 1 - k, last=True)
        yield
        out_ref[r, :, hf * W : (hf + 1) * W] = ring.total(acc8[0]).T.astype(BF)
        gat = Gather(cm, "z", r, lambda i: out_ref.at[i, :, cols])
        yield
        gat.run()

    halves = [chain(0), chain(1)]
    while halves:
        halves = [half for half in halves if next(half, True) is None]
    cm.drain()


def per_device(rhs_leaf, rhs_parent, inv_leaf, panel, row_map, inv_parent):
    rows, cols = inv_leaf.shape[1:]
    pb = panel.shape[1]
    R = rhs_leaf.shape[2]
    own = rhs_parent.shape[0]
    n8, blk, H = rows // 8, pb // 4, R // 2
    prow, pcol = inv_parent.shape
    V = pltpu.VMEM
    any_spec = pl.BlockSpec(memory_space=pl.ANY)
    vmem = pl.BlockSpec(memory_space=pltpu.VMEM)
    scratch = [
        V((rows, cols), BF), V((pb, rows), BF), V((prow, pcol), BF), V((cols, R), BF), V((own, R), BF),
        V((2, 4, n8, H), BF), V((2, 4, n8, H), BF), V((2, 4, n8, H), BF), V((2, n8, H), F32), V((2, 3, n8, H), BF),
        V((2, 4, 2, n8, H), BF), V((2, H, n8), BF),
        V((2, pb, H), F32), V((2, 32, 32, H), F32), V((2, 32, 32, H), BF), V((2, 32, 32, H), BF),
        V((2, 32, 32, H), BF), V((8, 32, own), F32), V((8, 32, own), F32),
        V((4 * own, 256), BF), V((256, 4 * own), BF), V((4, 256, blk), BF), V((4, blk, 256), BF),
        V((2, 4, own, H), BF), V((2, 3, own, H), BF), V((2, 4, 4, 2, own, H), BF),
        V((2, 4, own, H), BF), V((2, 3, own, H), BF), V((2, 4, H, own), BF),
        V((2, 4, 4, H, own), BF), V((2, 4, 4, H, own), BF), V((2, 4, 4, H, own), BF), V((2, 4, 4, H, own), F32),
        V((2, 3, 4, H, own), BF), V((2, 3, H, own), BF),
        V((2, 4, own, H), BF),
        V((2, 4, H, n8), BF), V((2, 4, H, n8), BF), V((2, 4, H, n8), BF), V((2, H, n8), F32), V((2, 3, H, n8), BF),
        V((2, 4, 2, H, n8), BF),
        V((2, 4, H, n8), F32), V((2, 4, H, n8), BF), V((2, 3, H, n8), BF),
        pltpu.SemaphoreType.DMA((160,)), pltpu.SemaphoreType.DMA((160,)), pltpu.SemaphoreType.DMA((12,)),
        pltpu.SemaphoreType.DMA((5,)), pltpu.SemaphoreType.DMA((5,)),
    ]
    sol_leaf, sol_parent = pl.pallas_call(
        kernel,
        out_shape=(
            jax.ShapeDtypeStruct((4, n8, R), BF),
            jax.ShapeDtypeStruct((own, R), BF),
        ),
        in_specs=[any_spec] * 5 + [vmem],
        out_specs=(vmem, vmem),
        scratch_shapes=scratch,
        compiler_params=pltpu.CompilerParams(
            collective_id=0, has_side_effects=True, vmem_limit_bytes=60 * 1024 * 1024
        ),
    )(
        rhs_leaf[0],
        rhs_parent,
        inv_leaf[0],
        panel[0],
        inv_parent,
        row_map[0].reshape(4, blk),
    )
    return (sol_leaf.reshape(1, 4 * n8, R), sol_parent)


def solution(mesh):
    in_specs = (
        P("leaf", "col", None),
        P(("leaf", "row", "col"), None),
        P("leaf", "row", "col"),
        P("leaf", "col", "row"),
        P("leaf", "col"),
        P(("row", "col"), "leaf"),
    )
    out_specs = (P("leaf", "col", None), P(("leaf", "row", "col"), None))
    return jax.shard_map(
        per_device, mesh=mesh, in_specs=in_specs, out_specs=out_specs, check_vma=False
    )
```

```python
import jax
import jax.numpy as jnp
from jax import lax
from jax.experimental import pallas as pl
from jax.experimental.pallas import tpu as pltpu
from jax.sharding import PartitionSpec as P

MESH = pl.DeviceIdType.MESH
BF = jnp.bfloat16
F32 = jnp.float32


def dot(a, b):
    return jnp.dot(a, b, preferred_element_type=F32)


class Comm:
    def __init__(self, ssem, rsem):
        self.ssem, self.rsem, self.n, self.sent = ssem, rsem, 0, []
        self.l, self.r, self.c = (lax.axis_index(a) for a in ("leaf", "row", "col"))
        self.x, self.k = self.c // 2, self.c % 2

    def at(self, axis, delta):
        if axis == "x":
            return (self.l, self.r, ((self.x + delta + 4) % 4) * 2 + self.k)
        if axis == "z":
            return (self.l, (self.r + delta + 4) % 4, self.c)
        if axis == "y":
            return ((self.l + delta + 4) % 4, self.r, self.c)
        return (self.l, self.r, self.x * 2 + 1 - self.k)

    def make(self, src, dst, device):
        at = self.n
        self.n += 1
        return pltpu.make_async_remote_copy(
            src_ref=src,
            dst_ref=dst,
            send_sem=self.ssem.at[at],
            recv_sem=self.rsem.at[at],
            device_id=device,
            device_id_type=MESH,
        )

    def send(self, src, dst, axis, delta=0):
        copy = self.make(src, dst, self.at(axis, delta))
        copy.start()
        self.sent.append(copy)
        return copy

    def drain(self):
        for copy in self.sent:
            copy.wait_send()
        self.sent = []


class Sum:
    def __init__(self, comm, axis, q, slot):
        self.comm, self.axis, self.q, self.slot, self.copies = comm, axis, q, slot, {}

    def put(self, d):
        self.copies[d] = self.comm.send(self.q(d), self.slot(d - 1), self.axis, d)

    def run(self):
        for d in (2, 1, 3):
            self.put(d)

    def total(self, own):
        for d in (1, 3, 2):
            self.copies[d].wait_recv()
            own = own + self.slot(d - 1)[...].astype(F32)
        return own


class Gather:
    def __init__(self, comm, axis, me, g):
        self.me = me
        self.copies = {d: comm.send(g(me), g(me), axis, d) for d in (2, 1, 3)}

    def wait(self, d):
        self.copies[d].wait_recv()
        return (self.me + 4 - d) % 4

    def run(self):
        for d in (1, 3, 2):
            self.wait(d)


def kernel(
    x_hbm, rp_hbm, a_hbm, b_hbm, p_hbm, rm_ref,
    out_ref, solp_ref,
    a_v, b_v, p_v, x_v, rp_v,
    sb1_, rb1_, q1_, own1_, rr1_, y_, yt_,
    u_acc_, g32_, g_, r1_, r2_, qs, qr, t1, t1t, s1, s1t,
    q3_, rr3_, gred_, q4_, rr4_, ft_,
    sb5_, rb5_, q5_, own5_, ra5_, rb5b_,
    sp_, sb7_, rb7_, q7_, own7_, rr7_, ct_,
    acc8_, q8_, rr8_,
    ssem, rsem, lsem, asem, bsem,
):
    cm = Comm(ssem, rsem)
    l, r, c, x, k = cm.l, cm.r, cm.c, cm.x, cm.k
    me = r * 8 + c
    n8 = y_.shape[3]
    W = x_v.shape[1] // 2
    own = rp_v.shape[0]
    blk = s1t.shape[1]
    order = ((1, 2), (1, 3), (0, 2), (1, 1), (0, 3), (1, 0), (0, 1), (0, 0))

    def a_rows(d, away):
        core = 1 - k if away else k
        return pl.ds(pl.multiple_of((((x + d) % 4) * 2 + core) * n8, n8), n8)

    loads = [pltpu.make_async_copy(x_hbm, x_v, lsem.at[0])]
    for i, (away, d) in enumerate(order):
        rows = a_rows(d, away)
        loads.append(pltpu.make_async_copy(a_hbm.at[rows], a_v.at[rows], lsem.at[1 + i]))
    loads.append(pltpu.make_async_copy(rp_hbm, rp_v, lsem.at[9]))
    loads.append(pltpu.make_async_copy(b_hbm, b_v, lsem.at[10]))
    loads.append(pltpu.make_async_copy(p_hbm, p_v, lsem.at[11]))
    for load in loads:
        load.start()
    loaded = set()

    def need(i):
        if i not in loaded:
            loaded.add(i)
            loads[i].wait()

    barrier = pltpu.get_barrier_semaphore()

    def greet(n, _):
        to = (me + n) % 32
        pl.semaphore_signal(barrier, inc=1, device_id=(l, to // 8, to % 8), device_id_type=MESH)
        return 0

    lax.fori_loop(1, 32, greet, 0)
    for d in (1, 2, 3):
        pl.semaphore_signal(barrier, inc=1, device_id=((l + d) % 4, r, c), device_id_type=MESH)

    def panel_cols(xx, core):
        return pl.ds(pl.multiple_of((xx * 2 + core) * n8, n8), n8)

    def row_wait():
        copy = pltpu.make_async_remote_copy(
            src_ref=qs.at[pl.ds(0, 7)], dst_ref=qr.at[pl.ds(0, 7)], send_sem=asem.at[0], recv_sem=bsem.at[0],
            device_id=cm.at("c", 0), device_id_type=MESH,
        )
        copy.wait_send()
        copy.wait_recv()

    def plane_exchange(src, src_at, dst, which):
        def one(n, _):
            to = (me + n) % 32
            pltpu.make_async_remote_copy(
                src_ref=src.at[src_at(to)], dst_ref=dst.at[me], send_sem=asem.at[which], recv_sem=bsem.at[which],
                device_id=(l, to // 8, to % 8), device_id_type=MESH,
            ).start()
            return 0

        lax.fori_loop(1, 32, one, 0)

    def plane_wait(dst, which):
        copy = pltpu.make_async_remote_copy(
            src_ref=dst.at[pl.ds(0, 31)], dst_ref=dst.at[pl.ds(0, 31)], send_sem=asem.at[which],
            recv_sem=bsem.at[which], device_id=cm.at("c", 0), device_id_type=MESH,
        )
        copy.wait_send()
        copy.wait_recv()

    def slot_tables():
        shift = own.bit_length() - 1
        before = lax.broadcasted_iota(jnp.int32, (blk, blk), 0) < lax.broadcasted_iota(jnp.int32, (blk, blk), 1)
        for i in range(4):
            e = rm_ref[0:1, i * blk : (i + 1) * blk]
            owner = lax.shift_right_logical(e, shift)
            local = lax.bitwise_and(e, own - 1).astype(F32)
            across = jnp.broadcast_to(owner.astype(F32), (blk, blk))
            rank = jnp.sum(jnp.where((across == across.T) & before, 1.0, 0.0), axis=0, keepdims=True)
            place = lax.bitwise_and(owner, 31) * 8 + lax.shift_right_logical(owner, 5) * 2
            place = place.astype(F32) + rank
            pick = jnp.where(
                lax.broadcasted_iota(jnp.int32, (256, blk), 0).astype(F32) == jnp.broadcast_to(place, (256, blk)),
                1.0,
                0.0,
            )
            s1[i] = pick.astype(BF)
            near = (lax.broadcasted_iota(jnp.int32, (64, blk), 0) + r * 64).astype(F32)
            where = jnp.where(near == jnp.broadcast_to(place, (64, blk)), jnp.broadcast_to(local + 1.0, (64, blk)), 0.0)
            qv = jnp.sum(where, axis=1, keepdims=True)
            qs[:, i * 8 : (i + 1) * 8, :] = jnp.broadcast_to(qv, (64, own)).reshape(8, 8, own)
        qr[pl.ds(c, 1)] = qs[pl.ds(c, 1)]
        for n in range(1, 8):
            to = (c + n) % 8
            pltpu.make_async_remote_copy(
                src_ref=qs.at[to], dst_ref=qr.at[c], send_sem=asem.at[0], recv_sem=bsem.at[0],
                device_id=(l, r, to), device_id_type=MESH,
            ).start()

    def parent_tables():
        row_wait()
        seen = qr[...].reshape(256, own)
        lane = lax.broadcasted_iota(jnp.int32, (256, own), 1).astype(F32) + 1.0
        leaf_of = lax.bitwise_and(
            lax.shift_right_logical(lax.broadcasted_iota(jnp.int32, (256, own), 0), 1), 3
        )
        for i in range(4):
            table = jnp.where((seen == lane) & (leaf_of == i), 1.0, 0.0)
            t1t[:, i * own : (i + 1) * own] = table.astype(BF)
            t1[i * own : (i + 1) * own, :] = table.T.astype(BF)

    def chain(hf):
        sb1, rb1, q1, own1, rr1, y_v, yt = (v.at[hf] for v in (sb1_, rb1_, q1_, own1_, rr1_, y_, yt_))
        u_acc, g32, g_v, r1_v, r2_v = (v.at[hf] for v in (u_acc_, g32_, g_, r1_, r2_))
        q3, rr3, gred, q4, rr4, ft = (v.at[hf] for v in (q3_, rr3_, gred_, q4_, rr4_, ft_))
        sb5, rb5, q5, own5, ra5, rb5b = (v.at[hf] for v in (sb5_, rb5_, q5_, own5_, ra5_, rb5b_))
        sp, sb7, rb7, q7, own7, rr7, ct = (v.at[hf] for v in (sp_, sb7_, rb7_, q7_, own7_, rr7_, ct_))
        acc8, q8, rr8 = (v.at[hf] for v in (acc8_, q8_, rr8_))
        cols = pl.ds(hf * W, W)

        sib = {}
        need(0)
        xv = x_v[:, hf * W : (hf + 1) * W]
        ring = Sum(cm, "x", lambda d: q1.at[d], lambda i: rr1.at[i])
        for i, (away, d) in enumerate(order):
            need(1 + i)
            part = dot(a_v[a_rows(d, away), :], xv)
            if away:
                sb1[d] = part.astype(BF)
                if hf == 0 and i == 0:
                    pl.semaphore_wait(barrier, 34)
                sib[d] = cm.send(sb1.at[d], rb1.at[d], "c")
                continue
            sib[d].wait_recv()
            part = part + rb1[d].astype(F32)
            if d:
                q1[d] = part.astype(BF)
                ring.put(d)
            else:
                own1[...] = part
        yield
        tot = ring.total(own1[...])
        y_v[x, k] = tot.astype(BF)

        fwd = {0: cm.send(y_v.at[x, k], y_v.at[x, k], "c")}
        gat = Gather(cm, "x", x, lambda i: y_v.at[i, k])
        yt[...] = tot.T.astype(BF)
        need(10)

        def push(xx, core, first=False):
            part = dot(b_v[:, panel_cols(xx, core)], y_v[xx, core])
            u_acc[...] = part if first else u_acc[...] + part

        push(x, k, True)
        yield
        if hf == 0:
            slot_tables()
        fwd[0].wait_recv()
        push(x, 1 - k)
        at = {}
        for d in (1, 3, 2):
            at[d] = gat.wait(d)
            fwd[d] = cm.send(y_v.at[at[d], k], y_v.at[at[d], k], "c")
        for d in (1, 3, 2):
            push(at[d], k)
        for d in (1, 3, 2):
            fwd[d].wait_recv()
            push(at[d], 1 - k)

        for i in range(4):
            rows = u_acc[i * blk : (i + 1) * blk].astype(BF)
            g32[:, i * 8 : (i + 1) * 8, :] = dot(s1[i], rows).reshape(32, 8, W)
        g_v[...] = g32[...].astype(BF)
        plane_exchange(g_v, lambda to: to, r1_v, 1 + 2 * hf)
        r1_v[pl.ds(me, 1)] = g_v[pl.ds(me, 1)]
        yield
        if hf == 0:
            parent_tables()
        plane_wait(r1_v, 1 + 2 * hf)
        got = r1_v[0:8].astype(F32)
        for i in range(1, 4):
            got = got + r1_v[8 * i : 8 * i + 8].astype(F32)
        got = got.reshape(256, W).astype(BF)

        def t_rows(d):
            return t1[pl.ds(pl.multiple_of(((l + d) % 4) * own, own), own), :]

        ring = Sum(cm, "y", lambda d: q3.at[d], lambda i: rr3.at[i])
        for d in (2, 1, 3):
            q3[d] = dot(t_rows(d), got).astype(BF)
            ring.put(d)
        tot = dot(t_rows(0), got)
        yield
        need(9)
        tot = rp_v[:, hf * W : (hf + 1) * W].astype(F32) - ring.total(tot)
        gred[r, x, k] = tot.astype(BF)

        if hf == 0:
            gat = Gather(cm, "x", x, lambda i: gred.at[r, i, k])
        else:
            gat = Gather(cm, "z", r, lambda i: gred.at[i, x, k])
            for i in range(4):
                s1t[i] = s1[i].astype(F32).T.astype(BF)
        yield
        gat.run()
        if hf == 0:
            part = lambda i: gred.at[i, :, k]
            gat = Gather(cm, "z", r, part)
            mine = r
        else:
            part = lambda i: gred.at[:, i, k]
            gat = Gather(cm, "x", x, part)
            mine = x
        fwd = [cm.send(part(mine), part(mine), "c")]
        need(11)
        yield
        for d in (1, 3, 2):
            i = gat.wait(d)
            fwd.append(cm.send(part(i), part(i), "c"))
        yield
        for copy in fwd:
            copy.wait_recv()
        parent = dot(p_v[...], gred[...].reshape(32 * own, W))
        u_acc[: 4 * own] = parent

        def f_rows(d):
            return u_acc[pl.ds(pl.multiple_of(((l + d) % 4) * own, own), own), :]

        ring = Sum(cm, "y", lambda d: q4.at[d], lambda i: rr4.at[i])
        for d in (2, 1, 3):
            q4[d] = f_rows(d).astype(BF)
            ring.put(d)
        yield
        ft[l] = ring.total(f_rows(0)).T.astype(BF)
        gat = Gather(cm, "y", l, lambda i: ft.at[i])
        yield
        gat.run()

        lhs = jnp.concatenate([ft[i] for i in range(4)], axis=1)
        sib = {}
        for dr in (2, 3, 1, 0):
            for dx in range(4):
                block = ((r + dr) % 4) * 4 + (x + dx) % 4
                part = dot(lhs, p_v[:, pl.ds(pl.multiple_of(block * 2 * own, 2 * own), 2 * own)])
                lo, hi = part[:, :own], part[:, own:]
                own5[dr, dx] = jnp.where(k == 0, lo, hi)
                sb5[dr, dx] = jnp.where(k == 0, hi, lo).astype(BF)
            sib[dr] = cm.send(sb5.at[dr], rb5.at[dr], "c")
        if hf == 0:
            ring = Sum(cm, "z", lambda d: q5.at[d], lambda i: ra5.at[i])
        else:
            ring = Sum(cm, "x", lambda d: q5.at[:, d], lambda i: ra5.at[i])
        for dr in (2, 3, 1, 0):
            sib[dr].wait_recv()
            tot = own5[dr] + rb5[dr].astype(F32)
            own5[dr] = tot
            q5[dr] = tot.astype(BF)
            if dr and hf == 0:
                ring.put(dr)
        if hf == 1:
            ring.run()
        yield
        if hf == 0:
            tot = ring.total(own5[0])
            q5[0] = tot.astype(BF)
            ring = Sum(cm, "x", lambda d: q5.at[0, d], lambda i: rb5b.at[i])
        else:
            tot = ring.total(own5[:, 0])
            q5[:, 0] = tot.astype(BF)
            ring = Sum(cm, "z", lambda d: q5.at[d, 0], lambda i: rb5b.at[i])
        ring.run()
        yield
        solved = ring.total(tot[0]).T.astype(BF)
        sp[l] = solved

        gat = Gather(cm, "y", l, lambda i: sp.at[i])
        solp_ref[:, hf * W : (hf + 1) * W] = solved
        yield
        gat.run()
        g_v[0:8] = dot(t1t[...], sp[...].reshape(4 * own, W)).astype(BF).reshape(8, 32, W)
        plane_exchange(g_v, lambda to: to % 8, r2_v, 2 + 2 * hf)
        r2_v[pl.ds(me, 1)] = g_v[pl.ds(c, 1)]
        yield
        plane_wait(r2_v, 2 + 2 * hf)
        g32[...] = r2_v[...].astype(F32)
        picked = jnp.concatenate(
            [dot(s1t[i], g32[:, i * 8 : (i + 1) * 8, :].reshape(256, W).astype(BF)) for i in range(4)], axis=0
        )
        picked = picked.T.astype(BF)

        sib = {}
        ring = Sum(cm, "x", lambda d: q7.at[d], lambda i: rr7.at[i])
        for away, d in order:
            part = dot(picked, b_v[:, panel_cols((x + d) % 4, 1 - k if away else k)])
            if away:
                sb7[d] = part.astype(BF)
                sib[d] = cm.send(sb7.at[d], rb7.at[d], "c")
                continue
            sib[d].wait_recv()
            part = part + rb7[d].astype(F32)
            if d:
                q7[d] = part.astype(BF)
                ring.put(d)
            else:
                own7[...] = part
        yield
        tot = ring.total(own7[...])
        ct[x, k] = (yt[...].astype(F32) - tot).astype(BF)

        fwd = {0: cm.send(ct.at[x, k], ct.at[x, k], "c")}
        gat = Gather(cm, "x", x, lambda i: ct.at[i, k])
        ring = Sum(cm, "z", lambda d: q8.at[d], lambda i: rr8.at[i])

        def pull(xx, core, first=False, last=False):
            lhs = ct[xx, core]
            rows = pl.ds(pl.multiple_of((xx * 2 + core) * n8, n8), n8)
            for d in (2, 1, 3, 0):
                part = dot(lhs, a_v[rows, pl.ds(pl.multiple_of(((r + d) % 4) * n8, n8), n8)])
                part = part if first else acc8[d] + part
                if last and d:
                    q8[d] = part.astype(BF)
                    ring.put(d)
                else:
                    acc8[d] = part

        pull(x, k, True)
        yield
        fwd[0].wait_recv()
        pull(x, 1 - k)
        at = {}
        for d in (1, 3, 2):
            at[d] = gat.wait(d)
            fwd[d] = cm.send(ct.at[at[d], k], ct.at[at[d], k], "c")
        for d in (1, 3, 2):
            pull(at[d], k)
        for d in (1, 3, 2):
            fwd[d].wait_recv()
            pull(at[d], 1 - k, last=d == 2)
        yield
        out_ref[r, :, hf * W : (hf + 1) * W] = ring.total(acc8[0]).T.astype(BF)
        gat = Gather(cm, "z", r, lambda i: out_ref.at[i, :, cols])
        yield
        gat.run()

    halves = [chain(0), chain(1)]
    while halves:
        halves = [half for half in halves if next(half, True) is None]
    cm.drain()


def per_device(rhs_leaf, rhs_parent, inv_leaf, panel, row_map, inv_parent):
    rows, cols = inv_leaf.shape[1:]
    pb = panel.shape[1]
    R = rhs_leaf.shape[2]
    own = rhs_parent.shape[0]
    n8, blk, H = rows // 8, pb // 4, R // 2
    prow, pcol = inv_parent.shape
    V = pltpu.VMEM
    any_spec = pl.BlockSpec(memory_space=pl.ANY)
    vmem = pl.BlockSpec(memory_space=pltpu.VMEM)
    scratch = [
        V((rows, cols), BF), V((pb, rows), BF), V((prow, pcol), BF), V((cols, R), BF), V((own, R), BF),
        V((2, 4, n8, H), BF), V((2, 4, n8, H), BF), V((2, 4, n8, H), BF), V((2, n8, H), F32), V((2, 3, n8, H), BF),
        V((2, 4, 2, n8, H), BF), V((2, H, n8), BF),
        V((2, pb, H), F32), V((2, 32, 32, H), F32), V((2, 32, 32, H), BF), V((2, 32, 32, H), BF),
        V((2, 32, 32, H), BF), V((8, 32, own), F32), V((8, 32, own), F32),
        V((4 * own, 256), BF), V((256, 4 * own), BF), V((4, 256, blk), BF), V((4, blk, 256), BF),
        V((2, 4, own, H), BF), V((2, 3, own, H), BF), V((2, 4, 4, 2, own, H), BF),
        V((2, 4, own, H), BF), V((2, 3, own, H), BF), V((2, 4, H, own), BF),
        V((2, 4, 4, H, own), BF), V((2, 4, 4, H, own), BF), V((2, 4, 4, H, own), BF), V((2, 4, 4, H, own), F32),
        V((2, 3, 4, H, own), BF), V((2, 3, H, own), BF),
        V((2, 4, own, H), BF),
        V((2, 4, H, n8), BF), V((2, 4, H, n8), BF), V((2, 4, H, n8), BF), V((2, H, n8), F32), V((2, 3, H, n8), BF),
        V((2, 4, 2, H, n8), BF),
        V((2, 4, H, n8), F32), V((2, 4, H, n8), BF), V((2, 3, H, n8), BF),
        pltpu.SemaphoreType.DMA((160,)), pltpu.SemaphoreType.DMA((160,)), pltpu.SemaphoreType.DMA((12,)),
        pltpu.SemaphoreType.DMA((5,)), pltpu.SemaphoreType.DMA((5,)),
    ]
    sol_leaf, sol_parent = pl.pallas_call(
        kernel,
        out_shape=(
            jax.ShapeDtypeStruct((4, n8, R), BF),
            jax.ShapeDtypeStruct((own, R), BF),
        ),
        in_specs=[any_spec] * 5 + [vmem],
        out_specs=(vmem, vmem),
        scratch_shapes=scratch,
        compiler_params=pltpu.CompilerParams(
            collective_id=0, has_side_effects=True, vmem_limit_bytes=60 * 1024 * 1024
        ),
    )(
        rhs_leaf[0],
        rhs_parent,
        inv_leaf[0],
        panel[0],
        inv_parent,
        row_map,
    )
    return (sol_leaf.reshape(1, 4 * n8, R), sol_parent)


def solution(mesh):
    in_specs = (
        P("leaf", "col", None),
        P(("leaf", "row", "col"), None),
        P("leaf", "row", "col"),
        P("leaf", "col", "row"),
        P("leaf", "col"),
        P(("row", "col"), "leaf"),
    )
    out_specs = (P("leaf", "col", None), P(("leaf", "row", "col"), None))
    return jax.shard_map(
        per_device, mesh=mesh, in_specs=in_specs, out_specs=out_specs, check_vma=False
    )
```

```python
import jax
import jax.numpy as jnp
from jax import lax
from jax.experimental import pallas as pl
from jax.experimental.pallas import tpu as pltpu
from jax.sharding import PartitionSpec as P

MESH = pl.DeviceIdType.MESH
BF = jnp.bfloat16
F32 = jnp.float32


def dot(a, b):
    return jnp.dot(a, b, preferred_element_type=F32)


class Comm:
    def __init__(self, ssem, rsem):
        self.ssem, self.rsem, self.n, self.sent = ssem, rsem, 0, []
        self.l, self.r, self.c = (lax.axis_index(a) for a in ("leaf", "row", "col"))
        self.x, self.k = self.c // 2, self.c % 2

    def at(self, axis, delta):
        if axis == "x":
            return (self.l, self.r, ((self.x + delta + 4) % 4) * 2 + self.k)
        if axis == "z":
            return (self.l, (self.r + delta + 4) % 4, self.c)
        if axis == "y":
            return ((self.l + delta + 4) % 4, self.r, self.c)
        return (self.l, self.r, self.x * 2 + 1 - self.k)

    def make(self, src, dst, device):
        at = self.n
        self.n += 1
        return pltpu.make_async_remote_copy(
            src_ref=src,
            dst_ref=dst,
            send_sem=self.ssem.at[at],
            recv_sem=self.rsem.at[at],
            device_id=device,
            device_id_type=MESH,
        )

    def send(self, src, dst, axis, delta=0):
        copy = self.make(src, dst, self.at(axis, delta))
        copy.start()
        self.sent.append(copy)
        return copy

    def drain(self):
        for copy in self.sent:
            copy.wait_send()
        self.sent = []


class Sum:
    def __init__(self, comm, axis, q, slot):
        self.comm, self.axis, self.q, self.slot, self.copies = comm, axis, q, slot, {}

    def put(self, d):
        self.copies[d] = self.comm.send(self.q(d), self.slot(d - 1), self.axis, d)

    def run(self):
        for d in (1, 3, 2):
            self.put(d)

    def total(self, own):
        for d in (1, 3, 2):
            self.copies[d].wait_recv()
            own = own + self.slot(d - 1)[...].astype(F32)
        return own


class Gather:
    def __init__(self, comm, axis, me, g):
        self.me = me
        self.copies = {d: comm.send(g(me), g(me), axis, d) for d in (1, 3, 2)}

    def wait(self, d):
        self.copies[d].wait_recv()
        return (self.me + 4 - d) % 4

    def run(self):
        for d in (1, 3, 2):
            self.wait(d)


def kernel(
    x_hbm, rp_hbm, a_hbm, b_hbm, p_hbm, rm_ref,
    out_ref, solp_ref,
    a_v, b_v, p_v, x_v, rp_v,
    sb1_, rb1_, q1_, own1_, rr1_, y_, yt_,
    u_acc_, g32_, g_, r1_, r2_, qs, qr, t1, t1t, s1, s1t,
    q3_, rr3_, gred_, q4_, rr4_, ft_,
    sb5_, rb5_, q5_, own5_, ra5_, rb5b_,
    sp_, sb7_, rb7_, q7_, own7_, rr7_, ct_,
    acc8_, q8_, rr8_,
    ssem, rsem, lsem, asem, bsem,
):
    cm = Comm(ssem, rsem)
    l, r, c, x, k = cm.l, cm.r, cm.c, cm.x, cm.k
    me = r * 8 + c
    n8 = y_.shape[3]
    W = x_v.shape[1] // 2
    own = rp_v.shape[0]
    blk = s1t.shape[1]
    order = ((1, 2), (1, 3), (1, 1), (1, 0), (0, 2), (0, 3), (0, 1), (0, 0))

    def a_rows(d, away):
        core = 1 - k if away else k
        return pl.ds(pl.multiple_of((((x + d) % 4) * 2 + core) * n8, n8), n8)

    loads = [pltpu.make_async_copy(x_hbm, x_v, lsem.at[0])]
    for i, (away, d) in enumerate(order):
        rows = a_rows(d, away)
        loads.append(pltpu.make_async_copy(a_hbm.at[rows], a_v.at[rows], lsem.at[1 + i]))
    loads.append(pltpu.make_async_copy(rp_hbm, rp_v, lsem.at[9]))
    loads.append(pltpu.make_async_copy(b_hbm, b_v, lsem.at[10]))
    loads.append(pltpu.make_async_copy(p_hbm, p_v, lsem.at[11]))
    for load in loads:
        load.start()
    loaded = set()

    def need(i):
        if i not in loaded:
            loaded.add(i)
            loads[i].wait()

    barrier = pltpu.get_barrier_semaphore()

    def greet(n, _):
        to = (me + n) % 32
        pl.semaphore_signal(barrier, inc=1, device_id=(l, to // 8, to % 8), device_id_type=MESH)
        return 0

    lax.fori_loop(1, 32, greet, 0)
    for d in (1, 2, 3):
        pl.semaphore_signal(barrier, inc=1, device_id=((l + d) % 4, r, c), device_id_type=MESH)

    def panel_cols(xx, core):
        return pl.ds(pl.multiple_of((xx * 2 + core) * n8, n8), n8)

    def row_wait():
        copy = pltpu.make_async_remote_copy(
            src_ref=qs.at[pl.ds(0, 7)], dst_ref=qr.at[pl.ds(0, 7)], send_sem=asem.at[0], recv_sem=bsem.at[0],
            device_id=cm.at("c", 0), device_id_type=MESH,
        )
        copy.wait_send()
        copy.wait_recv()

    def plane_exchange(src, src_at, dst, which):
        def one(n, _):
            to = (me + n) % 32
            pltpu.make_async_remote_copy(
                src_ref=src.at[src_at(to)], dst_ref=dst.at[me], send_sem=asem.at[which], recv_sem=bsem.at[which],
                device_id=(l, to // 8, to % 8), device_id_type=MESH,
            ).start()
            return 0

        lax.fori_loop(1, 32, one, 0)

    def plane_wait(dst, which):
        copy = pltpu.make_async_remote_copy(
            src_ref=dst.at[pl.ds(0, 31)], dst_ref=dst.at[pl.ds(0, 31)], send_sem=asem.at[which],
            recv_sem=bsem.at[which], device_id=cm.at("c", 0), device_id_type=MESH,
        )
        copy.wait_send()
        copy.wait_recv()

    def slot_tables():
        shift = own.bit_length() - 1
        before = lax.broadcasted_iota(jnp.int32, (blk, blk), 0) < lax.broadcasted_iota(jnp.int32, (blk, blk), 1)
        for i in range(4):
            e = rm_ref[0:1, i * blk : (i + 1) * blk]
            owner = lax.shift_right_logical(e, shift)
            local = lax.bitwise_and(e, own - 1).astype(F32)
            across = jnp.broadcast_to(owner.astype(F32), (blk, blk))
            rank = jnp.sum(jnp.where((across == across.T) & before, 1.0, 0.0), axis=0, keepdims=True)
            place = lax.bitwise_and(owner, 31) * 8 + lax.shift_right_logical(owner, 5) * 2
            place = place.astype(F32) + rank
            pick = jnp.where(
                lax.broadcasted_iota(jnp.int32, (256, blk), 0).astype(F32) == jnp.broadcast_to(place, (256, blk)),
                1.0,
                0.0,
            )
            s1[i] = pick.astype(BF)
            near = (lax.broadcasted_iota(jnp.int32, (64, blk), 0) + r * 64).astype(F32)
            where = jnp.where(near == jnp.broadcast_to(place, (64, blk)), jnp.broadcast_to(local + 1.0, (64, blk)), 0.0)
            qv = jnp.sum(where, axis=1, keepdims=True)
            qs[:, i * 8 : (i + 1) * 8, :] = jnp.broadcast_to(qv, (64, own)).reshape(8, 8, own)
        qr[pl.ds(c, 1)] = qs[pl.ds(c, 1)]
        for n in range(1, 8):
            to = (c + n) % 8
            pltpu.make_async_remote_copy(
                src_ref=qs.at[to], dst_ref=qr.at[c], send_sem=asem.at[0], recv_sem=bsem.at[0],
                device_id=(l, r, to), device_id_type=MESH,
            ).start()

    def parent_tables():
        row_wait()
        seen = qr[...].reshape(256, own)
        lane = lax.broadcasted_iota(jnp.int32, (256, own), 1).astype(F32) + 1.0
        leaf_of = lax.bitwise_and(
            lax.shift_right_logical(lax.broadcasted_iota(jnp.int32, (256, own), 0), 1), 3
        )
        for i in range(4):
            table = jnp.where((seen == lane) & (leaf_of == i), 1.0, 0.0)
            t1t[:, i * own : (i + 1) * own] = table.astype(BF)
            t1[i * own : (i + 1) * own, :] = table.T.astype(BF)

    def chain(hf):
        sb1, rb1, q1, own1, rr1, y_v, yt = (v.at[hf] for v in (sb1_, rb1_, q1_, own1_, rr1_, y_, yt_))
        u_acc, g32, g_v, r1_v, r2_v = (v.at[hf] for v in (u_acc_, g32_, g_, r1_, r2_))
        q3, rr3, gred, q4, rr4, ft = (v.at[hf] for v in (q3_, rr3_, gred_, q4_, rr4_, ft_))
        sb5, rb5, q5, own5, ra5, rb5b = (v.at[hf] for v in (sb5_, rb5_, q5_, own5_, ra5_, rb5b_))
        sp, sb7, rb7, q7, own7, rr7, ct = (v.at[hf] for v in (sp_, sb7_, rb7_, q7_, own7_, rr7_, ct_))
        acc8, q8, rr8 = (v.at[hf] for v in (acc8_, q8_, rr8_))
        cols = pl.ds(hf * W, W)

        sib = {}
        need(0)
        xv = x_v[:, hf * W : (hf + 1) * W]
        ring = Sum(cm, "x", lambda d: q1.at[d], lambda i: rr1.at[i])
        for i, (away, d) in enumerate(order):
            need(1 + i)
            part = dot(a_v[a_rows(d, away), :], xv)
            if away:
                sb1[d] = part.astype(BF)
                if hf == 0 and i == 0:
                    pl.semaphore_wait(barrier, 34)
                sib[d] = cm.send(sb1.at[d], rb1.at[d], "c")
                continue
            sib[d].wait_recv()
            part = part + rb1[d].astype(F32)
            if d:
                q1[d] = part.astype(BF)
                ring.put(d)
            else:
                own1[...] = part
        yield
        tot = ring.total(own1[...])
        y_v[x, k] = tot.astype(BF)

        fwd = {0: cm.send(y_v.at[x, k], y_v.at[x, k], "c")}
        gat = Gather(cm, "x", x, lambda i: y_v.at[i, k])
        yt[...] = tot.T.astype(BF)
        need(10)

        def push(xx, core, first=False):
            part = dot(b_v[:, panel_cols(xx, core)], y_v[xx, core])
            u_acc[...] = part if first else u_acc[...] + part

        push(x, k, True)
        yield
        if hf == 0:
            slot_tables()
        fwd[0].wait_recv()
        push(x, 1 - k)
        at = {}
        for d in (1, 3, 2):
            at[d] = gat.wait(d)
            fwd[d] = cm.send(y_v.at[at[d], k], y_v.at[at[d], k], "c")
        for d in (1, 3, 2):
            push(at[d], k)
        for d in (1, 3, 2):
            fwd[d].wait_recv()
            push(at[d], 1 - k)

        for i in range(4):
            rows = u_acc[i * blk : (i + 1) * blk].astype(BF)
            g32[:, i * 8 : (i + 1) * 8, :] = dot(s1[i], rows).reshape(32, 8, W)
        g_v[...] = g32[...].astype(BF)
        plane_exchange(g_v, lambda to: to, r1_v, 1 + 2 * hf)
        r1_v[pl.ds(me, 1)] = g_v[pl.ds(me, 1)]
        yield
        if hf == 0:
            parent_tables()
        plane_wait(r1_v, 1 + 2 * hf)
        got = r1_v[0:8].astype(F32)
        for i in range(1, 4):
            got = got + r1_v[8 * i : 8 * i + 8].astype(F32)
        got = got.reshape(256, W).astype(BF)

        def t_rows(d):
            return t1[pl.ds(pl.multiple_of(((l + d) % 4) * own, own), own), :]

        ring = Sum(cm, "y", lambda d: q3.at[d], lambda i: rr3.at[i])
        for d in (2, 1, 3):
            q3[d] = dot(t_rows(d), got).astype(BF)
            ring.put(d)
        tot = dot(t_rows(0), got)
        yield
        need(9)
        tot = rp_v[:, hf * W : (hf + 1) * W].astype(F32) - ring.total(tot)
        gred[r, x, k] = tot.astype(BF)

        if hf == 0:
            gat = Gather(cm, "x", x, lambda i: gred.at[r, i, k])
        else:
            gat = Gather(cm, "z", r, lambda i: gred.at[i, x, k])
            for i in range(4):
                s1t[i] = s1[i].astype(F32).T.astype(BF)
        yield
        gat.run()
        if hf == 0:
            part = lambda i: gred.at[i, :, k]
            gat = Gather(cm, "z", r, part)
            mine = r
        else:
            part = lambda i: gred.at[:, i, k]
            gat = Gather(cm, "x", x, part)
            mine = x
        fwd = [cm.send(part(mine), part(mine), "c")]
        need(11)
        yield
        for d in (1, 3, 2):
            i = gat.wait(d)
            fwd.append(cm.send(part(i), part(i), "c"))
        yield
        for copy in fwd:
            copy.wait_recv()
        parent = dot(p_v[...], gred[...].reshape(32 * own, W))
        u_acc[: 4 * own] = parent

        def f_rows(d):
            return u_acc[pl.ds(pl.multiple_of(((l + d) % 4) * own, own), own), :]

        ring = Sum(cm, "y", lambda d: q4.at[d], lambda i: rr4.at[i])
        for d in (2, 1, 3):
            q4[d] = f_rows(d).astype(BF)
            ring.put(d)
        yield
        ft[l] = ring.total(f_rows(0)).T.astype(BF)
        gat = Gather(cm, "y", l, lambda i: ft.at[i])
        yield
        gat.run()

        lhs = jnp.concatenate([ft[i] for i in range(4)], axis=1)
        sib = {}
        for dr in (2, 3, 1, 0):
            for dx in range(4):
                block = ((r + dr) % 4) * 4 + (x + dx) % 4
                part = dot(lhs, p_v[:, pl.ds(pl.multiple_of(block * 2 * own, 2 * own), 2 * own)])
                lo, hi = part[:, :own], part[:, own:]
                own5[dr, dx] = jnp.where(k == 0, lo, hi)
                sb5[dr, dx] = jnp.where(k == 0, hi, lo).astype(BF)
            sib[dr] = cm.send(sb5.at[dr], rb5.at[dr], "c")
        if hf == 0:
            ring = Sum(cm, "z", lambda d: q5.at[d], lambda i: ra5.at[i])
        else:
            ring = Sum(cm, "x", lambda d: q5.at[:, d], lambda i: ra5.at[i])
        for dr in (2, 3, 1, 0):
            sib[dr].wait_recv()
            tot = own5[dr] + rb5[dr].astype(F32)
            own5[dr] = tot
            q5[dr] = tot.astype(BF)
            if dr and hf == 0:
                ring.put(dr)
        if hf == 1:
            ring.run()
        yield
        if hf == 0:
            tot = ring.total(own5[0])
            q5[0] = tot.astype(BF)
            ring = Sum(cm, "x", lambda d: q5.at[0, d], lambda i: rb5b.at[i])
        else:
            tot = ring.total(own5[:, 0])
            q5[:, 0] = tot.astype(BF)
            ring = Sum(cm, "z", lambda d: q5.at[d, 0], lambda i: rb5b.at[i])
        ring.run()
        yield
        solved = ring.total(tot[0]).T.astype(BF)
        sp[l] = solved

        gat = Gather(cm, "y", l, lambda i: sp.at[i])
        solp_ref[:, hf * W : (hf + 1) * W] = solved
        yield
        gat.run()
        g_v[0:8] = dot(t1t[...], sp[...].reshape(4 * own, W)).astype(BF).reshape(8, 32, W)
        plane_exchange(g_v, lambda to: to % 8, r2_v, 2 + 2 * hf)
        r2_v[pl.ds(me, 1)] = g_v[pl.ds(c, 1)]
        yield
        plane_wait(r2_v, 2 + 2 * hf)
        g32[...] = r2_v[...].astype(F32)
        picked = jnp.concatenate(
            [dot(s1t[i], g32[:, i * 8 : (i + 1) * 8, :].reshape(256, W).astype(BF)) for i in range(4)], axis=0
        )
        picked = picked.T.astype(BF)

        sib = {}
        ring = Sum(cm, "x", lambda d: q7.at[d], lambda i: rr7.at[i])
        for away, d in order:
            part = dot(picked, b_v[:, panel_cols((x + d) % 4, 1 - k if away else k)])
            if away:
                sb7[d] = part.astype(BF)
                sib[d] = cm.send(sb7.at[d], rb7.at[d], "c")
                continue
            sib[d].wait_recv()
            part = part + rb7[d].astype(F32)
            if d:
                q7[d] = part.astype(BF)
                ring.put(d)
            else:
                own7[...] = part
        yield
        tot = ring.total(own7[...])
        ct[x, k] = (yt[...].astype(F32) - tot).astype(BF)

        fwd = {0: cm.send(ct.at[x, k], ct.at[x, k], "c")}
        gat = Gather(cm, "x", x, lambda i: ct.at[i, k])
        ring = Sum(cm, "z", lambda d: q8.at[d], lambda i: rr8.at[i])

        def pull(xx, core, first=False, last=False):
            lhs = ct[xx, core]
            rows = pl.ds(pl.multiple_of((xx * 2 + core) * n8, n8), n8)
            for d in (2, 1, 3, 0):
                part = dot(lhs, a_v[rows, pl.ds(pl.multiple_of(((r + d) % 4) * n8, n8), n8)])
                part = part if first else acc8[d] + part
                if last and d:
                    q8[d] = part.astype(BF)
                    ring.put(d)
                else:
                    acc8[d] = part

        pull(x, k, True)
        yield
        fwd[0].wait_recv()
        pull(x, 1 - k)
        at = {}
        for d in (1, 3, 2):
            at[d] = gat.wait(d)
            fwd[d] = cm.send(ct.at[at[d], k], ct.at[at[d], k], "c")
        for d in (1, 3, 2):
            pull(at[d], k)
        for d in (1, 3, 2):
            fwd[d].wait_recv()
            pull(at[d], 1 - k, last=d == 2)
        yield
        out_ref[r, :, hf * W : (hf + 1) * W] = ring.total(acc8[0]).T.astype(BF)
        gat = Gather(cm, "z", r, lambda i: out_ref.at[i, :, cols])
        yield
        gat.run()

    halves = [chain(0), chain(1)]
    while halves:
        halves = [half for half in halves if next(half, True) is None]
    cm.drain()


def per_device(rhs_leaf, rhs_parent, inv_leaf, panel, row_map, inv_parent):
    rows, cols = inv_leaf.shape[1:]
    pb = panel.shape[1]
    R = rhs_leaf.shape[2]
    own = rhs_parent.shape[0]
    n8, blk, H = rows // 8, pb // 4, R // 2
    prow, pcol = inv_parent.shape
    V = pltpu.VMEM
    any_spec = pl.BlockSpec(memory_space=pl.ANY)
    vmem = pl.BlockSpec(memory_space=pltpu.VMEM)
    scratch = [
        V((rows, cols), BF), V((pb, rows), BF), V((prow, pcol), BF), V((cols, R), BF), V((own, R), BF),
        V((2, 4, n8, H), BF), V((2, 4, n8, H), BF), V((2, 4, n8, H), BF), V((2, n8, H), F32), V((2, 3, n8, H), BF),
        V((2, 4, 2, n8, H), BF), V((2, H, n8), BF),
        V((2, pb, H), F32), V((2, 32, 32, H), F32), V((2, 32, 32, H), BF), V((2, 32, 32, H), BF),
        V((2, 32, 32, H), BF), V((8, 32, own), F32), V((8, 32, own), F32),
        V((4 * own, 256), BF), V((256, 4 * own), BF), V((4, 256, blk), BF), V((4, blk, 256), BF),
        V((2, 4, own, H), BF), V((2, 3, own, H), BF), V((2, 4, 4, 2, own, H), BF),
        V((2, 4, own, H), BF), V((2, 3, own, H), BF), V((2, 4, H, own), BF),
        V((2, 4, 4, H, own), BF), V((2, 4, 4, H, own), BF), V((2, 4, 4, H, own), BF), V((2, 4, 4, H, own), F32),
        V((2, 3, 4, H, own), BF), V((2, 3, H, own), BF),
        V((2, 4, own, H), BF),
        V((2, 4, H, n8), BF), V((2, 4, H, n8), BF), V((2, 4, H, n8), BF), V((2, H, n8), F32), V((2, 3, H, n8), BF),
        V((2, 4, 2, H, n8), BF),
        V((2, 4, H, n8), F32), V((2, 4, H, n8), BF), V((2, 3, H, n8), BF),
        pltpu.SemaphoreType.DMA((160,)), pltpu.SemaphoreType.DMA((160,)), pltpu.SemaphoreType.DMA((12,)),
        pltpu.SemaphoreType.DMA((5,)), pltpu.SemaphoreType.DMA((5,)),
    ]
    sol_leaf, sol_parent = pl.pallas_call(
        kernel,
        out_shape=(
            jax.ShapeDtypeStruct((4, n8, R), BF),
            jax.ShapeDtypeStruct((own, R), BF),
        ),
        in_specs=[any_spec] * 5 + [vmem],
        out_specs=(vmem, vmem),
        scratch_shapes=scratch,
        compiler_params=pltpu.CompilerParams(
            collective_id=0, has_side_effects=True, vmem_limit_bytes=60 * 1024 * 1024
        ),
    )(
        rhs_leaf[0],
        rhs_parent,
        inv_leaf[0],
        panel[0],
        inv_parent,
        row_map,
    )
    return (sol_leaf.reshape(1, 4 * n8, R), sol_parent)


def solution(mesh):
    in_specs = (
        P("leaf", "col", None),
        P(("leaf", "row", "col"), None),
        P("leaf", "row", "col"),
        P("leaf", "col", "row"),
        P("leaf", "col"),
        P(("row", "col"), "leaf"),
    )
    out_specs = (P("leaf", "col", None), P(("leaf", "row", "col"), None))
    return jax.shard_map(
        per_device, mesh=mesh, in_specs=in_specs, out_specs=out_specs, check_vma=False
    )
```

```python
import jax
import jax.numpy as jnp
from jax import lax
from jax.experimental import pallas as pl
from jax.experimental.pallas import tpu as pltpu
from jax.sharding import PartitionSpec as P

MESH = pl.DeviceIdType.MESH
BF = jnp.bfloat16
F32 = jnp.float32


def dot(a, b):
    return jnp.dot(a, b, preferred_element_type=F32)


class Comm:
    def __init__(self, ssem, rsem):
        self.ssem, self.rsem, self.n, self.sent = ssem, rsem, 0, []
        self.l, self.r, self.c = (lax.axis_index(a) for a in ("leaf", "row", "col"))
        self.x, self.k = self.c // 2, self.c % 2

    def at(self, axis, delta):
        if axis == "x":
            return (self.l, self.r, ((self.x + delta + 4) % 4) * 2 + self.k)
        if axis == "z":
            return (self.l, (self.r + delta + 4) % 4, self.c)
        if axis == "y":
            return ((self.l + delta + 4) % 4, self.r, self.c)
        return (self.l, self.r, self.x * 2 + 1 - self.k)

    def make(self, src, dst, device):
        at = self.n
        self.n += 1
        return pltpu.make_async_remote_copy(
            src_ref=src,
            dst_ref=dst,
            send_sem=self.ssem.at[at],
            recv_sem=self.rsem.at[at],
            device_id=device,
            device_id_type=MESH,
        )

    def send(self, src, dst, axis, delta=0):
        copy = self.make(src, dst, self.at(axis, delta))
        copy.start()
        self.sent.append(copy)
        return copy

    def drain(self):
        for copy in self.sent:
            copy.wait_send()
        self.sent = []


class Sum:
    def __init__(self, comm, axis, q, slot):
        self.comm, self.axis, self.q, self.slot, self.copies = comm, axis, q, slot, {}

    def put(self, d):
        self.copies[d] = self.comm.send(self.q(d), self.slot(d - 1), self.axis, d)

    def run(self):
        for d in (1, 3, 2):
            self.put(d)

    def total(self, own):
        for d in (1, 3, 2):
            self.copies[d].wait_recv()
            own = own + self.slot(d - 1)[...].astype(F32)
        return own


class Gather:
    def __init__(self, comm, axis, me, g):
        self.me = me
        self.copies = {d: comm.send(g(me), g(me), axis, d) for d in (1, 3, 2)}

    def wait(self, d):
        self.copies[d].wait_recv()
        return (self.me + 4 - d) % 4

    def run(self):
        for d in (1, 3, 2):
            self.wait(d)


def kernel(
    x_hbm, rp_hbm, a_hbm, b_hbm, p_hbm, rm_ref,
    out_ref, solp_ref,
    a_v, b_v, p_v, x_v, rp_v,
    sb1_, rb1_, q1_, own1_, rr1_, y_, yt_,
    u_acc_, g32_, g_, r1_, r2_, qs, qr, t1, t1t, s1, s1t,
    q3_, rr3_, gred_, q4_, rr4_, ft_,
    sb5_, rb5_, q5_, own5_, ra5_, rb5b_,
    sp_, sb7_, rb7_, q7_, own7_, rr7_, ct_,
    acc8_, q8_, rr8_,
    ssem, rsem, lsem, asem, bsem,
):
    cm = Comm(ssem, rsem)
    l, r, c, x, k = cm.l, cm.r, cm.c, cm.x, cm.k
    me = r * 8 + c
    n8 = y_.shape[3]
    W = x_v.shape[1] // 2
    own = rp_v.shape[0]
    blk = s1t.shape[1]
    order = ((1, 2), (1, 3), (1, 1), (1, 0), (0, 2), (0, 3), (0, 1), (0, 0))

    def a_rows(d, away):
        core = 1 - k if away else k
        return pl.ds(pl.multiple_of((((x + d) % 4) * 2 + core) * n8, n8), n8)

    loads = [pltpu.make_async_copy(x_hbm, x_v, lsem.at[0])]
    for i, (away, d) in enumerate(order):
        rows = a_rows(d, away)
        loads.append(pltpu.make_async_copy(a_hbm.at[rows], a_v.at[rows], lsem.at[1 + i]))
    loads.append(pltpu.make_async_copy(rp_hbm, rp_v, lsem.at[9]))
    loads.append(pltpu.make_async_copy(b_hbm, b_v, lsem.at[10]))
    loads.append(pltpu.make_async_copy(p_hbm, p_v, lsem.at[11]))
    for load in loads:
        load.start()
    loaded = set()

    def need(i):
        if i not in loaded:
            loaded.add(i)
            loads[i].wait()

    barrier = pltpu.get_barrier_semaphore()

    def greet(n, _):
        to = (me + n) % 32
        pl.semaphore_signal(barrier, inc=1, device_id=(l, to // 8, to % 8), device_id_type=MESH)
        return 0

    lax.fori_loop(1, 32, greet, 0)
    for d in (1, 2, 3):
        pl.semaphore_signal(barrier, inc=1, device_id=((l + d) % 4, r, c), device_id_type=MESH)

    def panel_cols(xx, core):
        return pl.ds(pl.multiple_of((xx * 2 + core) * n8, n8), n8)

    def row_wait():
        copy = pltpu.make_async_remote_copy(
            src_ref=qs.at[pl.ds(0, 7)], dst_ref=qr.at[pl.ds(0, 7)], send_sem=asem.at[0], recv_sem=bsem.at[0],
            device_id=cm.at("c", 0), device_id_type=MESH,
        )
        copy.wait_send()
        copy.wait_recv()

    def plane_exchange(src, src_at, dst, which):
        def one(n, _):
            to = (me + n) % 32
            pltpu.make_async_remote_copy(
                src_ref=src.at[src_at(to)], dst_ref=dst.at[me], send_sem=asem.at[which], recv_sem=bsem.at[which],
                device_id=(l, to // 8, to % 8), device_id_type=MESH,
            ).start()
            return 0

        lax.fori_loop(1, 32, one, 0)

    def plane_wait(dst, which):
        copy = pltpu.make_async_remote_copy(
            src_ref=dst.at[pl.ds(0, 31)], dst_ref=dst.at[pl.ds(0, 31)], send_sem=asem.at[which],
            recv_sem=bsem.at[which], device_id=cm.at("c", 0), device_id_type=MESH,
        )
        copy.wait_send()
        copy.wait_recv()

    def slot_tables():
        shift = own.bit_length() - 1
        before = lax.broadcasted_iota(jnp.int32, (blk, blk), 0) < lax.broadcasted_iota(jnp.int32, (blk, blk), 1)
        for i in range(4):
            e = rm_ref[0:1, i * blk : (i + 1) * blk]
            owner = lax.shift_right_logical(e, shift)
            local = lax.bitwise_and(e, own - 1).astype(F32)
            across = jnp.broadcast_to(owner.astype(F32), (blk, blk))
            rank = jnp.sum(jnp.where((across == across.T) & before, 1.0, 0.0), axis=0, keepdims=True)
            place = lax.bitwise_and(owner, 31) * 8 + lax.shift_right_logical(owner, 5) * 2
            place = place.astype(F32) + rank
            pick = jnp.where(
                lax.broadcasted_iota(jnp.int32, (256, blk), 0).astype(F32) == jnp.broadcast_to(place, (256, blk)),
                1.0,
                0.0,
            )
            s1[i] = pick.astype(BF)
            s1t[i] = pick.T.astype(BF)
            near = (lax.broadcasted_iota(jnp.int32, (64, blk), 0) + r * 64).astype(F32)
            where = jnp.where(near == jnp.broadcast_to(place, (64, blk)), jnp.broadcast_to(local + 1.0, (64, blk)), 0.0)
            qv = jnp.sum(where, axis=1, keepdims=True)
            qs[:, i * 8 : (i + 1) * 8, :] = jnp.broadcast_to(qv, (64, own)).reshape(8, 8, own)
        qr[pl.ds(c, 1)] = qs[pl.ds(c, 1)]
        for n in range(1, 8):
            to = (c + n) % 8
            pltpu.make_async_remote_copy(
                src_ref=qs.at[to], dst_ref=qr.at[c], send_sem=asem.at[0], recv_sem=bsem.at[0],
                device_id=(l, r, to), device_id_type=MESH,
            ).start()

    def parent_tables():
        row_wait()
        seen = qr[...].reshape(256, own)
        lane = lax.broadcasted_iota(jnp.int32, (256, own), 1).astype(F32) + 1.0
        leaf_of = lax.bitwise_and(
            lax.shift_right_logical(lax.broadcasted_iota(jnp.int32, (256, own), 0), 1), 3
        )
        for i in range(4):
            table = jnp.where((seen == lane) & (leaf_of == i), 1.0, 0.0)
            t1t[:, i * own : (i + 1) * own] = table.astype(BF)
            t1[i * own : (i + 1) * own, :] = table.T.astype(BF)

    def chain(hf):
        sb1, rb1, q1, own1, rr1, y_v, yt = (v.at[hf] for v in (sb1_, rb1_, q1_, own1_, rr1_, y_, yt_))
        u_acc, g32, g_v, r1_v, r2_v = (v.at[hf] for v in (u_acc_, g32_, g_, r1_, r2_))
        q3, rr3, gred, q4, rr4, ft = (v.at[hf] for v in (q3_, rr3_, gred_, q4_, rr4_, ft_))
        sb5, rb5, q5, own5, ra5, rb5b = (v.at[hf] for v in (sb5_, rb5_, q5_, own5_, ra5_, rb5b_))
        sp, sb7, rb7, q7, own7, rr7, ct = (v.at[hf] for v in (sp_, sb7_, rb7_, q7_, own7_, rr7_, ct_))
        acc8, q8, rr8 = (v.at[hf] for v in (acc8_, q8_, rr8_))
        cols = pl.ds(hf * W, W)

        sib = {}
        need(0)
        xv = x_v[:, hf * W : (hf + 1) * W]
        ring = Sum(cm, "x", lambda d: q1.at[d], lambda i: rr1.at[i])
        for i, (away, d) in enumerate(order):
            need(1 + i)
            part = dot(a_v[a_rows(d, away), :], xv)
            if away:
                sb1[d] = part.astype(BF)
                if hf == 0 and i == 0:
                    pl.semaphore_wait(barrier, 34)
                sib[d] = cm.send(sb1.at[d], rb1.at[d], "c")
                continue
            sib[d].wait_recv()
            part = part + rb1[d].astype(F32)
            if d:
                q1[d] = part.astype(BF)
                ring.put(d)
            else:
                own1[...] = part
        yield
        tot = ring.total(own1[...])
        y_v[x, k] = tot.astype(BF)

        fwd = {0: cm.send(y_v.at[x, k], y_v.at[x, k], "c")}
        gat = Gather(cm, "x", x, lambda i: y_v.at[i, k])
        need(10)

        def push(xx, core, first=False):
            part = dot(b_v[:, panel_cols(xx, core)], y_v[xx, core])
            u_acc[...] = part if first else u_acc[...] + part

        yield
        if hf == 0:
            slot_tables()
        yt[...] = tot.T.astype(BF)
        push(x, k, True)
        fwd[0].wait_recv()
        push(x, 1 - k)
        at = {}
        for d in (1, 3, 2):
            at[d] = gat.wait(d)
            fwd[d] = cm.send(y_v.at[at[d], k], y_v.at[at[d], k], "c")
        for d in (1, 3, 2):
            push(at[d], k)
        for d in (1, 3, 2):
            fwd[d].wait_recv()
            push(at[d], 1 - k)

        for i in range(4):
            rows = u_acc[i * blk : (i + 1) * blk].astype(BF)
            g32[:, i * 8 : (i + 1) * 8, :] = dot(s1[i], rows).reshape(32, 8, W)
        g_v[...] = g32[...].astype(BF)
        plane_exchange(g_v, lambda to: to, r1_v, 1 + 2 * hf)
        r1_v[pl.ds(me, 1)] = g_v[pl.ds(me, 1)]
        yield
        if hf == 0:
            parent_tables()
        plane_wait(r1_v, 1 + 2 * hf)
        got = r1_v[0:8].astype(F32)
        for i in range(1, 4):
            got = got + r1_v[8 * i : 8 * i + 8].astype(F32)
        got = got.reshape(256, W).astype(BF)

        def t_rows(d):
            return t1[pl.ds(pl.multiple_of(((l + d) % 4) * own, own), own), :]

        ring = Sum(cm, "y", lambda d: q3.at[d], lambda i: rr3.at[i])
        for d in (2, 1, 3):
            q3[d] = dot(t_rows(d), got).astype(BF)
            ring.put(d)
        tot = dot(t_rows(0), got)
        yield
        need(9)
        tot = rp_v[:, hf * W : (hf + 1) * W].astype(F32) - ring.total(tot)
        gred[r, x, k] = tot.astype(BF)

        if hf == 0:
            gat = Gather(cm, "x", x, lambda i: gred.at[r, i, k])
        else:
            gat = Gather(cm, "z", r, lambda i: gred.at[i, x, k])
        yield
        gat.run()
        if hf == 0:
            part = lambda i: gred.at[i, :, k]
            gat = Gather(cm, "z", r, part)
            mine = r
        else:
            part = lambda i: gred.at[:, i, k]
            gat = Gather(cm, "x", x, part)
            mine = x
        fwd = [cm.send(part(mine), part(mine), "c")]
        need(11)
        yield
        for d in (1, 3, 2):
            i = gat.wait(d)
            fwd.append(cm.send(part(i), part(i), "c"))
        yield
        for copy in fwd:
            copy.wait_recv()
        parent = dot(p_v[...], gred[...].reshape(32 * own, W))
        u_acc[: 4 * own] = parent

        def f_rows(d):
            return u_acc[pl.ds(pl.multiple_of(((l + d) % 4) * own, own), own), :]

        ring = Sum(cm, "y", lambda d: q4.at[d], lambda i: rr4.at[i])
        for d in (2, 1, 3):
            q4[d] = f_rows(d).astype(BF)
            ring.put(d)
        yield
        ft[l] = ring.total(f_rows(0)).T.astype(BF)
        gat = Gather(cm, "y", l, lambda i: ft.at[i])
        yield
        gat.run()

        lhs = jnp.concatenate([ft[i] for i in range(4)], axis=1)
        sib = {}
        for dr in (2, 3, 1, 0):
            for dx in range(4):
                block = ((r + dr) % 4) * 4 + (x + dx) % 4
                part = dot(lhs, p_v[:, pl.ds(pl.multiple_of(block * 2 * own, 2 * own), 2 * own)])
                lo, hi = part[:, :own], part[:, own:]
                own5[dr, dx] = jnp.where(k == 0, lo, hi)
                sb5[dr, dx] = jnp.where(k == 0, hi, lo).astype(BF)
            sib[dr] = cm.send(sb5.at[dr], rb5.at[dr], "c")
        if hf == 0:
            ring = Sum(cm, "z", lambda d: q5.at[d], lambda i: ra5.at[i])
        else:
            ring = Sum(cm, "x", lambda d: q5.at[:, d], lambda i: ra5.at[i])
        for dr in (2, 3, 1, 0):
            sib[dr].wait_recv()
            tot = own5[dr] + rb5[dr].astype(F32)
            own5[dr] = tot
            q5[dr] = tot.astype(BF)
            if dr and hf == 0:
                ring.put(dr)
        if hf == 1:
            ring.run()
        yield
        if hf == 0:
            tot = ring.total(own5[0])
            q5[0] = tot.astype(BF)
            ring = Sum(cm, "x", lambda d: q5.at[0, d], lambda i: rb5b.at[i])
        else:
            tot = ring.total(own5[:, 0])
            q5[:, 0] = tot.astype(BF)
            ring = Sum(cm, "z", lambda d: q5.at[d, 0], lambda i: rb5b.at[i])
        ring.run()
        yield
        solved = ring.total(tot[0]).T.astype(BF)
        sp[l] = solved

        gat = Gather(cm, "y", l, lambda i: sp.at[i])
        yield
        solp_ref[:, hf * W : (hf + 1) * W] = solved
        gat.run()
        g_v[0:8] = dot(t1t[...], sp[...].reshape(4 * own, W)).astype(BF).reshape(8, 32, W)
        plane_exchange(g_v, lambda to: to % 8, r2_v, 2 + 2 * hf)
        r2_v[pl.ds(me, 1)] = g_v[pl.ds(c, 1)]
        yield
        plane_wait(r2_v, 2 + 2 * hf)
        g32[...] = r2_v[...].astype(F32)
        picked = jnp.concatenate(
            [dot(s1t[i], g32[:, i * 8 : (i + 1) * 8, :].reshape(256, W).astype(BF)) for i in range(4)], axis=0
        )
        picked = picked.T.astype(BF)

        sib = {}
        ring = Sum(cm, "x", lambda d: q7.at[d], lambda i: rr7.at[i])
        for away, d in order:
            part = dot(picked, b_v[:, panel_cols((x + d) % 4, 1 - k if away else k)])
            if away:
                sb7[d] = part.astype(BF)
                sib[d] = cm.send(sb7.at[d], rb7.at[d], "c")
                continue
            sib[d].wait_recv()
            part = part + rb7[d].astype(F32)
            if d:
                q7[d] = part.astype(BF)
                ring.put(d)
            else:
                own7[...] = part
        yield
        tot = ring.total(own7[...])
        ct[x, k] = (yt[...].astype(F32) - tot).astype(BF)

        fwd = {0: cm.send(ct.at[x, k], ct.at[x, k], "c")}
        gat = Gather(cm, "x", x, lambda i: ct.at[i, k])
        ring = Sum(cm, "z", lambda d: q8.at[d], lambda i: rr8.at[i])

        def pull(xx, core, first=False, last=False):
            lhs = ct[xx, core]
            rows = pl.ds(pl.multiple_of((xx * 2 + core) * n8, n8), n8)
            for d in (2, 1, 3, 0):
                part = dot(lhs, a_v[rows, pl.ds(pl.multiple_of(((r + d) % 4) * n8, n8), n8)])
                part = part if first else acc8[d] + part
                if last and d:
                    q8[d] = part.astype(BF)
                    ring.put(d)
                else:
                    acc8[d] = part

        yield
        pull(x, k, True)
        fwd[0].wait_recv()
        pull(x, 1 - k)
        at = {}
        for d in (1, 3, 2):
            at[d] = gat.wait(d)
            fwd[d] = cm.send(ct.at[at[d], k], ct.at[at[d], k], "c")
        for d in (1, 3, 2):
            pull(at[d], k)
        for d in (1, 3, 2):
            fwd[d].wait_recv()
            pull(at[d], 1 - k, last=d == 2)
        yield
        out_ref[r, :, hf * W : (hf + 1) * W] = ring.total(acc8[0]).T.astype(BF)
        gat = Gather(cm, "z", r, lambda i: out_ref.at[i, :, cols])
        yield
        gat.run()

    halves = [chain(0), chain(1)]
    while halves:
        halves = [half for half in halves if next(half, True) is None]
    cm.drain()


def per_device(rhs_leaf, rhs_parent, inv_leaf, panel, row_map, inv_parent):
    rows, cols = inv_leaf.shape[1:]
    pb = panel.shape[1]
    R = rhs_leaf.shape[2]
    own = rhs_parent.shape[0]
    n8, blk, H = rows // 8, pb // 4, R // 2
    prow, pcol = inv_parent.shape
    V = pltpu.VMEM
    any_spec = pl.BlockSpec(memory_space=pl.ANY)
    vmem = pl.BlockSpec(memory_space=pltpu.VMEM)
    scratch = [
        V((rows, cols), BF), V((pb, rows), BF), V((prow, pcol), BF), V((cols, R), BF), V((own, R), BF),
        V((2, 4, n8, H), BF), V((2, 4, n8, H), BF), V((2, 4, n8, H), BF), V((2, n8, H), F32), V((2, 3, n8, H), BF),
        V((2, 4, 2, n8, H), BF), V((2, H, n8), BF),
        V((2, pb, H), F32), V((2, 32, 32, H), F32), V((2, 32, 32, H), BF), V((2, 32, 32, H), BF),
        V((2, 32, 32, H), BF), V((8, 32, own), F32), V((8, 32, own), F32),
        V((4 * own, 256), BF), V((256, 4 * own), BF), V((4, 256, blk), BF), V((4, blk, 256), BF),
        V((2, 4, own, H), BF), V((2, 3, own, H), BF), V((2, 4, 4, 2, own, H), BF),
        V((2, 4, own, H), BF), V((2, 3, own, H), BF), V((2, 4, H, own), BF),
        V((2, 4, 4, H, own), BF), V((2, 4, 4, H, own), BF), V((2, 4, 4, H, own), BF), V((2, 4, 4, H, own), F32),
        V((2, 3, 4, H, own), BF), V((2, 3, H, own), BF),
        V((2, 4, own, H), BF),
        V((2, 4, H, n8), BF), V((2, 4, H, n8), BF), V((2, 4, H, n8), BF), V((2, H, n8), F32), V((2, 3, H, n8), BF),
        V((2, 4, 2, H, n8), BF),
        V((2, 4, H, n8), F32), V((2, 4, H, n8), BF), V((2, 3, H, n8), BF),
        pltpu.SemaphoreType.DMA((160,)), pltpu.SemaphoreType.DMA((160,)), pltpu.SemaphoreType.DMA((12,)),
        pltpu.SemaphoreType.DMA((5,)), pltpu.SemaphoreType.DMA((5,)),
    ]
    sol_leaf, sol_parent = pl.pallas_call(
        kernel,
        out_shape=(
            jax.ShapeDtypeStruct((4, n8, R), BF),
            jax.ShapeDtypeStruct((own, R), BF),
        ),
        in_specs=[any_spec] * 5 + [vmem],
        out_specs=(vmem, vmem),
        scratch_shapes=scratch,
        compiler_params=pltpu.CompilerParams(
            collective_id=0, has_side_effects=True, vmem_limit_bytes=60 * 1024 * 1024
        ),
    )(
        rhs_leaf[0],
        rhs_parent,
        inv_leaf[0],
        panel[0],
        inv_parent,
        row_map,
    )
    return (sol_leaf.reshape(1, 4 * n8, R), sol_parent)


def solution(mesh):
    in_specs = (
        P("leaf", "col", None),
        P(("leaf", "row", "col"), None),
        P("leaf", "row", "col"),
        P("leaf", "col", "row"),
        P("leaf", "col"),
        P(("row", "col"), "leaf"),
    )
    out_specs = (P("leaf", "col", None), P(("leaf", "row", "col"), None))
    return jax.shard_map(
        per_device, mesh=mesh, in_specs=in_specs, out_specs=out_specs, check_vma=False
    )
```
